32 devices in a mesh: fields: 2 (over x), seq: 8 (over z, y), head: 2 (over core).
Axes of the slice: x: 2, y: 2, z: 4, core: 2. Of those that a mesh axis runs over, the one named last changes fastest.
Arguments:
- tokens: bfloat16 [65536, 512], P(('fields', 'seq')), parts along dimension 0, may hold values from -6 to 6
- norm_gain: float32 [512], replicated, may hold values from 0.1 to 1.9
- coarse_gain: float32 [512], replicated, may hold values from 0.25 to 2.5
- w_query: bfloat16 [512, 512], P(None, 'head'), may hold values from -0.25 to 0.25
- w_key: bfloat16 [512, 512], P(None, 'head'), may hold values from -0.25 to 0.25
- w_value: bfloat16 [512, 512], P(None, 'head'), may hold values from -0.25 to 0.25
- w_out: bfloat16 [512, 512], replicated, may hold values from -0.25 to 0.25
- score_scale: float32 [8], P('head'), may hold values from 1 to 40, as said below
Outputs:
- attn_out: bfloat16 [65536, 512], P(('fields', 'seq'), 'head'), parts along dimension 0
The draws below stay inside these ranges and needn't reach their ends.
There are 2 independent parts, one for each index of `fields`. The reference program is written for one: setup_inputs(seed, part) draws one part's arguments, and reference() takes and returns one part's arrays. A program takes and returns all parts, laid end to end along the dimension named above; an argument that names none is the same for every part. Nothing has to cross between parts.
Inputs may be any that keep to these rules, and one draw needn't show every extreme that they name: `score_scale`: per-head score temperature.
All inputs are finite; a program needn't handle non-finite values.
Results may differ from the reference program's by a relative error of at most 0.0035.
The reference program's roundings to bfloat16 on the way count: a program that leaves them out, or rounds other values in their place, can miss the bound.
Values may be sent and summed in bfloat16 or wider, within the bound.
No kernel may reach another device: no remote copies, remote signals or barrier semaphores. Data moves between devices by JAX's collectives and lax.ppermute only.
A program may use at most 64 MiB of HBM per device.

```python
import math
import jax
import jax.numpy as jnp
from jax import lax

D = 512
HEADS = 8
HEAD_DIM = 64
WINDOW = 256
POOL = 1024
QB = 512
TOKENS = 32768
COARSE = 32


def draw_score_scale(key, part):
    return jnp.exp(jax.random.uniform(key, (HEADS,), jnp.float32, 0.0, math.log(4.0)))


def steps_of(key, extent, cuts, smallest, top_value):
    gain, own = 1.0, jax.random.fold_in(key, 6)
    for axis_at, parts in cuts:
        draws = jnp.exp(jax.random.uniform(jax.random.fold_in(own, axis_at), (parts,), jnp.float32, smallest / len(cuts), top_value / len(cuts)))
        gain = gain * jnp.repeat(draws, extent[axis_at] // parts).reshape([-1 if axis == axis_at else 1 for axis in range(len(extent))])
    return gain


def bell_draw(key, dims, width, most, cuts=(), held_as=jnp.bfloat16):
    drawn = width * jax.random.normal(key, dims, jnp.float32)
    if cuts:
        drawn = drawn * steps_of(key, dims, cuts, -0.22, 0.18)
    return jnp.clip(drawn, -most, most).astype(held_as)


def setup_inputs(seed: int = 0, part: int = 0) -> dict:
    keys = jax.random.split(jax.random.key(seed), 9)
    own_keys = jax.random.split(jax.random.fold_in(keys[8], part), 9)
    return {
        "tokens": bell_draw(own_keys[0], (TOKENS, D), 1.0, 6.0, ((0, 8),)),
        "norm_gain": jnp.clip(1.0 + 0.18 * jax.random.normal(keys[1], (D,), jnp.float32), 0.1, 1.9),
        "coarse_gain": jnp.clip(jnp.exp(jax.random.uniform(keys[2], (D,), jnp.float32, math.log(0.25), math.log(2.5))), 0.25, 2.5),
        "w_query": bell_draw(keys[3], (D, D), D ** -0.5, 0.25, ((1, 2),)),
        "w_key": bell_draw(keys[4], (D, D), D ** -0.5, 0.25, ((1, 2),)),
        "w_value": bell_draw(keys[5], (D, D), D ** -0.5, 0.25, ((1, 2),)),
        "w_out": bell_draw(keys[6], (D, D), D ** -0.5, 0.25),
        "score_scale": draw_score_scale(jax.random.fold_in(keys[8], 71), part),
    }


def rms_rows(matrix, scaling):
    return matrix * lax.rsqrt(lax.optimization_barrier(jnp.mean(matrix * matrix, axis=-1, keepdims=True)) + 1e-05) * scaling

def unit_heads(matrix, head_count):
    split = matrix.reshape(matrix.shape[0], head_count, HEAD_DIM)
    return split * lax.rsqrt(lax.optimization_barrier(jnp.mean(split * split, axis=-1, keepdims=True)) + 1e-06)

def reference(tokens, norm_gain, coarse_gain, w_query, w_key, w_value, w_out, score_scale):
    normed = rms_rows(tokens.astype(jnp.float32), norm_gain.astype(jnp.float32)).astype(jnp.bfloat16)
    factor = (score_scale.astype(jnp.float32) * HEAD_DIM ** (-0.5))[None, :, None]
    queries = (unit_heads(jnp.dot(normed, w_query, preferred_element_type=jnp.float32), HEADS) * factor).astype(jnp.bfloat16)
    key_rows = unit_heads(jnp.dot(normed, w_key, preferred_element_type=jnp.float32), HEADS).astype(jnp.bfloat16)
    value_rows = jnp.dot(normed, w_value, preferred_element_type=jnp.float32).astype(jnp.bfloat16)
    value_rows = value_rows.reshape(TOKENS, HEADS, HEAD_DIM)
    normed_kept = lax.optimization_barrier(normed)
    pooled = lax.optimization_barrier(jnp.mean(normed_kept.astype(jnp.float32).reshape(COARSE, POOL, D), axis=1))
    coarse = rms_rows(pooled, coarse_gain.astype(jnp.float32)).astype(jnp.bfloat16)
    coarse_keys = unit_heads(jnp.dot(coarse, w_key, preferred_element_type=jnp.float32), HEADS).astype(jnp.bfloat16)
    coarse_values = jnp.dot(coarse, w_value, preferred_element_type=jnp.float32).astype(jnp.bfloat16)
    coarse_values = coarse_values.reshape(COARSE, HEADS, HEAD_DIM)
    queries, key_rows, value_rows, coarse_keys, coarse_values = lax.optimization_barrier((queries, key_rows, value_rows, coarse_keys, coarse_values))
    padded_keys = jnp.pad(key_rows, ((WINDOW, WINDOW), (0, 0), (0, 0)))
    padded_values = jnp.pad(value_rows, ((WINDOW, WINDOW), (0, 0), (0, 0)))
    far_keys = coarse_keys.astype(jnp.float32)
    far_values = coarse_values.astype(jnp.float32)
    span = QB + 2 * WINDOW
    offsets = jnp.arange(QB, dtype=jnp.int32)[:, None] - jnp.arange(span, dtype=jnp.int32)[None, :] + WINDOW
    near = jnp.abs(offsets) <= WINDOW

    def one_block(block_id):
        row_start = block_id * QB
        block_queries = lax.dynamic_slice_in_dim(queries, row_start, QB, 0).astype(jnp.float32)
        block_keys = lax.dynamic_slice_in_dim(padded_keys, row_start, span, 0).astype(jnp.float32)
        block_values = lax.dynamic_slice_in_dim(padded_values, row_start, span, 0).astype(jnp.float32)
        band = jnp.einsum('qhd,khd->hqk', block_queries, block_keys)
        positions = row_start + jnp.arange(span, dtype=jnp.int32) - WINDOW
        inside = (positions >= 0) & (positions < TOKENS)
        band = jnp.where(near[None] & inside[None, None, :], band, -1e+30)
        far = jnp.einsum('qhd,khd->hqk', block_queries, far_keys)
        peak = jnp.maximum(lax.optimization_barrier(jnp.max(band, axis=-1, keepdims=True)), lax.optimization_barrier(jnp.max(far, axis=-1, keepdims=True)))
        band_exp = jnp.exp(band - peak)
        far_exp = jnp.exp(far - peak)
        total = lax.optimization_barrier(jnp.sum(band_exp, axis=-1, keepdims=True)) + lax.optimization_barrier(jnp.sum(far_exp, axis=-1, keepdims=True))
        band_weights = (band_exp / total).astype(jnp.bfloat16)
        far_weights = (far_exp / total).astype(jnp.bfloat16)
        band_weights, far_weights = lax.optimization_barrier((band_weights, far_weights))
        mixed = jnp.einsum('hqk,khd->qhd', band_weights.astype(jnp.float32), block_values)
        mixed = mixed + jnp.einsum('hqk,khd->qhd', far_weights.astype(jnp.float32), far_values)
        return mixed.astype(jnp.bfloat16).reshape(QB, D)
    blocks = lax.map(one_block, jnp.arange(TOKENS // QB, dtype=jnp.int32))
    attended = blocks.reshape(TOKENS, D)
    return jnp.dot(attended, w_out, preferred_element_type=jnp.float32).astype(jnp.bfloat16)
```

```python
import functools

import jax
import jax.numpy as jnp
from jax import lax
from jax.experimental import pallas as pl
from jax.experimental.pallas import tpu as pltpu
from jax.sharding import PartitionSpec as P

HEAD_DIM = 64
WINDOW = 256
POOL = 1024
BQ = 128
SPAN = BQ + 2 * WINDOW
TILES = SPAN // 128
STRIP = 16
NORM_ROWS = 512
PROJ_ROWS = 512
HIDDEN = -1e30
CHUNKS = 2

VMEM = pl.BlockSpec(memory_space=pltpu.VMEM)
ANY = pl.BlockSpec(memory_space=pl.ANY)
BF16 = jnp.bfloat16
F32 = jnp.float32


def sds(shape, dtype):
    return jax.ShapeDtypeStruct(shape, dtype)


def dot(a, b):
    return jnp.dot(a, b, preferred_element_type=F32)


def call(kernel, outs, *args, in_specs=None, out_specs=None, scratch=(), limit=24, flops=0, name=None):
    cost = pl.CostEstimate(flops=flops, bytes_accessed=4 << 20, transcendentals=0)
    return pl.pallas_call(
        kernel,
        out_shape=outs,
        in_specs=in_specs or [VMEM] * len(args),
        out_specs=out_specs or jax.tree.map(lambda _: VMEM, outs),
        scratch_shapes=scratch,
        compiler_params=pltpu.CompilerParams(vmem_limit_bytes=limit << 20),
        cost_estimate=cost,
        name=name,
    )(*args)


def rms(x, gain):
    return x * lax.rsqrt(jnp.mean(x * x, axis=-1, keepdims=True) + 1e-05) * gain


def unit(x, ones_ref):
    square = x * x
    high = square.astype(BF16)
    low = (square - high.astype(F32)).astype(BF16)
    mean = dot(high, ones_ref[...]) + dot(low, ones_ref[...])
    return x * lax.rsqrt(mean + 1e-06)


def norm_kernel(tok_ref, gain_ref, coarse_gain_ref, normed_ref, coarse_ref, buf, sems):
    rows = tok_ref.shape[0]
    count = rows // NORM_ROWS
    copies = []
    for c in range(count):
        part = pl.ds(c * NORM_ROWS, NORM_ROWS)
        copies.append(pltpu.make_async_copy(tok_ref.at[part], buf.at[part], sems.at[c]))
        copies[-1].start()
    gain = gain_ref[...]
    ones = jnp.ones((8, NORM_ROWS), BF16)
    pooled = []
    for c in range(count):
        part = pl.ds(c * NORM_ROWS, NORM_ROWS)
        copies[c].wait()
        normed = rms(buf[part, :].astype(F32), gain).astype(BF16)
        normed_ref[part, :] = normed
        total = dot(ones, normed)[:1]
        if c * NORM_ROWS % POOL:
            pooled[-1] = pooled[-1] + total
        else:
            pooled.append(total)
    pooled = jnp.concatenate(pooled, 0) * (1.0 / POOL)
    coarse_ref[...] = rms(pooled, coarse_gain_ref[...]).astype(BF16)


def query_kernel(normed_ref, w_ref, ones_ref, factor_ref, q_ref):
    @pl.loop(0, normed_ref.shape[0] // PROJ_ROWS)
    def _(c):
        part = pl.ds(pl.multiple_of(c * PROJ_ROWS, PROJ_ROWS), PROJ_ROWS)
        q = unit(dot(normed_ref[part, :], w_ref[...]), ones_ref) * factor_ref[...]
        q_ref[part, :] = q.astype(BF16)


def key_value_kernel(
    normed_ref, mine_ref, other_ref, gain_ref, wk_ref, wv_ref, ones_ref, k_ref, v_ref
):
    rows = normed_ref.shape[0]
    half = WINDOW // 2

    @pl.loop(0, rows // PROJ_ROWS)
    def _(c):
        part = pl.ds(pl.multiple_of(c * PROJ_ROWS, PROJ_ROWS), PROJ_ROWS)
        out = pl.ds(pl.multiple_of(c * PROJ_ROWS + WINDOW, WINDOW), PROJ_ROWS)
        normed = normed_ref[part, :]
        k_ref[out, :] = unit(dot(normed, wk_ref[...]), ones_ref).astype(BF16)
        v_ref[out, :] = dot(normed, wv_ref[...]).astype(BF16)

    far = jnp.concatenate([mine_ref[...], other_ref[...]], 0)
    normed = rms(far.astype(F32), gain_ref[...]).astype(BF16)
    keys = unit(dot(normed, wk_ref[...]), ones_ref).astype(BF16)
    values = dot(normed, wv_ref[...]).astype(BF16)
    odd = lax.axis_index("seq") % 2
    core = lax.axis_index("head")
    for piece in range(4):
        at_low = odd if piece % 2 == 0 else 1 - odd
        side = core if piece < 2 else 1 - core
        start = jnp.where(at_low == 1, 0, rows + WINDOW) + side * half
        out = pl.ds(pl.multiple_of(start, half), half)
        k_ref[out, :] = keys[piece * half : (piece + 1) * half]
        v_ref[out, :] = values[piece * half : (piece + 1) * half]


def attention_kernel(
    base, q_ref, k_ref, v_ref, coarse_ref, wk_ref, wv_ref, ones_ref, o_ref, s_ref, p_ref, far_ref
):
    blocks = o_ref.shape[0] // BQ
    width = q_ref.shape[1]
    heads = width // HEAD_DIM
    stack = heads * BQ
    far_count = coarse_ref.shape[0]
    far_width = far_ref.shape[1]
    far_tiles = far_width // 128
    tiles = TILES + far_tiles
    all_blocks = q_ref.shape[0] // BQ
    lane_head = lax.broadcasted_iota(jnp.int32, (BQ, width), 1) // HEAD_DIM
    seq_index = lax.axis_index("seq")
    is_first = seq_index == 0
    is_last = seq_index == lax.axis_size("seq") - 1

    far_ref[...] = jnp.zeros_like(far_ref)
    coarse = coarse_ref[...]
    far_ref[0, :far_count, :] = unit(dot(coarse, wk_ref[...]), ones_ref).astype(BF16)
    far_ref[1, :far_count, :] = dot(coarse, wv_ref[...]).astype(BF16)

    def rows_at(b, size):
        return pl.ds(pl.multiple_of(base + b * BQ, BQ), size)

    def scores(b, slot):
        q = q_ref[rows_at(b, BQ), :]
        queries = jnp.concatenate(
            [jnp.where(lane_head == h, q, jnp.zeros_like(q)) for h in range(heads)], 0
        )
        keys = jnp.concatenate([k_ref[rows_at(b, SPAN), :], far_ref[0]], 0)
        s_ref[slot] = lax.dot_general(
            queries, keys, (((1,), (1,)), ((), ())), preferred_element_type=F32
        )

    def hide_outside(b, slot):
        block = base // BQ + b
        for edge, distance, near, outer in (
            (is_first, block, 1, 0),
            (is_last, all_blocks - 1 - block, TILES - 2, TILES - 1),
        ):
            for tile, reach in ((near, 1), (outer, 2)):

                @pl.when(edge & (distance < reach))
                def _():
                    s_ref[slot, :, tile * 128 : tile * 128 + 128] = jnp.full(
                        (stack, 128), HIDDEN, F32
                    )

    def softmax(slot):
        lane = lax.broadcasted_iota(jnp.int32, (STRIP, 128), 1)
        ahead = lane - lax.broadcasted_iota(jnp.int32, (STRIP, 128), 0)
        for r in range(0, stack, STRIP):
            at = r % BQ
            part = [s_ref[slot, r : r + STRIP, 128 * t : 128 * t + 128] for t in range(tiles)]
            part[0] = jnp.where(ahead >= at, part[0], HIDDEN)
            part[TILES - 1] = jnp.where(ahead <= at, part[TILES - 1], HIDDEN)
            if far_count < far_width:
                used = far_count - (far_tiles - 1) * 128
                part[-1] = jnp.where(lane < used, part[-1], HIDDEN)
            peak = jnp.max(functools.reduce(jnp.maximum, part), axis=1, keepdims=True)
            part = [jnp.exp(x - peak) for x in part]
            total = jnp.sum(functools.reduce(jnp.add, part), axis=1, keepdims=True)
            scale = 1.0 / total
            for t in range(tiles):
                p_ref[slot, r : r + STRIP, 128 * t : 128 * t + 128] = (part[t] * scale).astype(BF16)

    def mix(b, slot):
        values = jnp.concatenate([v_ref[rows_at(b, SPAN), :], far_ref[1]], 0)
        mixed = dot(p_ref[slot], values)
        out = mixed[:BQ]
        for h in range(1, heads):
            out = jnp.where(lane_head == h, mixed[h * BQ : (h + 1) * BQ], out)
        o_ref[pl.ds(pl.multiple_of(b * BQ, BQ), BQ), :] = out.astype(BF16)

    scores(0, 0)

    @pl.loop(0, blocks // 2)
    def _(i):
        for slot in range(2):
            b = 2 * i + slot
            hide_outside(b, slot)
            mix(jnp.maximum(b - 1, 0), 1 - slot)
            scores(jnp.minimum(b + 1, blocks - 1), 1 - slot)
            softmax(slot)

    mix(blocks - 1, 1)


def out_kernel(own_ref, other_ref, w_ref, *rest):
    o_ref = rest[-1]
    core = lax.axis_index("head")
    width = own_ref.shape[1]

    def weight(rows_of):
        rows = pl.ds(pl.multiple_of(rows_of * width, width), width)
        return w_ref[rows, pl.ds(pl.multiple_of(core * width, width), width)]

    out = dot(own_ref[...], weight(core)) + dot(other_ref[...], weight(1 - core))
    o_ref[...] = out.astype(BF16)


def swap_heads(x):
    return lax.ppermute(x, "head", [(0, 1), (1, 0)])


def halo_rows(tokens, seq_size):
    rows = tokens.shape[0]
    half = WINDOW // 2
    even = lax.axis_index("seq") % 2 == 0
    side = lax.axis_index("head") * half
    first = lax.dynamic_slice_in_dim(tokens, jnp.where(even, rows - WINDOW, 0) + side, half, 0)
    second = lax.dynamic_slice_in_dim(tokens, jnp.where(even, 0, rows - WINDOW) + side, half, 0)
    moved = []
    for block, start in ((first, 0), (second, 1)):
        pairs = [(i, i + 1) for i in range(start, seq_size - 1, 2)]
        pairs = pairs + [(b, a) for a, b in pairs]
        moved.append(lax.ppermute(block, "seq", pairs))
    mine = jnp.concatenate(moved, 0)
    return mine, swap_heads(mine)


def gather_rows(rows, seq_size):
    if seq_size & (seq_size - 1):
        return lax.all_gather(rows, "seq", axis=0, tiled=True)
    step = 1
    while step < seq_size:
        pairs = [(i, i ^ step) for i in range(seq_size)]
        rows = jnp.concatenate([rows, lax.ppermute(rows, "seq", pairs)], 0)
        step *= 2
    return rows


def body(tokens, norm_gain, coarse_gain, w_query, w_key, w_value, w_out, score_scale):
    rows, full = tokens.shape
    heads = score_scale.shape[0]
    width = heads * HEAD_DIM
    seq_size = lax.axis_size("seq")
    gain = norm_gain[None]
    lane_head = jnp.arange(width) // HEAD_DIM
    ones = jnp.where(lane_head[:, None] == lane_head[None], 1.0 / HEAD_DIM, 0.0).astype(BF16)
    factor = jnp.repeat(score_scale * HEAD_DIM ** (-0.5), HEAD_DIM)[None]

    mine, other = halo_rows(tokens, seq_size)
    normed, coarse = call(
        norm_kernel,
        (sds((rows, full), BF16), sds((rows // POOL, full), BF16)),
        tokens,
        gain,
        coarse_gain[None],
        in_specs=[ANY, VMEM, VMEM],
        scratch=[
            pltpu.VMEM((rows, full), BF16),
            pltpu.SemaphoreType.DMA((rows // NORM_ROWS,)),
        ],
        flops=2 << 30,
        name="norm",
    )
    coarse_all = gather_rows(coarse, seq_size)
    queries = call(
        query_kernel,
        sds((rows, width), BF16),
        normed,
        w_query,
        ones,
        factor,
        flops=2 << 30,
        name="queries",
    )
    keys, values = call(
        key_value_kernel,
        (sds((rows + 2 * WINDOW, width), BF16),) * 2,
        normed,
        mine,
        other,
        gain,
        w_key,
        w_value,
        ones,
        flops=4 << 30,
        name="keys_values",
    )
    far_width = -(-coarse_all.shape[0] // 128) * 128
    chunk = rows // CHUNKS
    stack = heads * BQ
    out = ()
    for c in range(CHUNKS):
        attended = call(
            functools.partial(attention_kernel, c * chunk),
            sds((chunk, width), BF16),
            queries,
            keys,
            values,
            coarse_all,
            w_key,
            w_value,
            ones,
            scratch=[
                pltpu.VMEM((2, stack, SPAN + far_width), F32),
                pltpu.VMEM((2, stack, SPAN + far_width), BF16),
                pltpu.VMEM((2, far_width, width), BF16),
            ],
            flops=10 << 30,
            name="attention",
        )
        swapped = swap_heads(attended)
        first = c * chunk // PROJ_ROWS
        block = pl.BlockSpec((PROJ_ROWS, width), lambda i: (i, 0))
        out = pl.pallas_call(
            out_kernel,
            out_shape=sds((rows, width), BF16),
            grid=(chunk // PROJ_ROWS,),
            in_specs=[block, block, pl.BlockSpec((full, full), lambda i: (0, 0))] + [ANY] * (c > 0),
            out_specs=pl.BlockSpec((PROJ_ROWS, width), lambda i, first=first: (first + i, 0)),
            input_output_aliases={3: 0} if c else {},
            cost_estimate=pl.CostEstimate(
                flops=1 << 30, bytes_accessed=4 << 20, transcendentals=0
            ),
            name="out",
        )(attended, swapped, w_out, *([out] if c else []))
    return out


def solution(mesh):
    return jax.shard_map(
        body,
        mesh=mesh,
        in_specs=(
            P(("fields", "seq"), None),
            P(),
            P(),
            P(None, "head"),
            P(None, "head"),
            P(None, "head"),
            P(),
            P("head"),
        ),
        out_specs=P(("fields", "seq"), "head"),
        check_vma=False,
    )
```

```python
import functools

import jax
import jax.numpy as jnp
from jax import lax
from jax.experimental import pallas as pl
from jax.experimental.pallas import tpu as pltpu
from jax.sharding import PartitionSpec as P

HEAD_DIM = 64
WINDOW = 256
POOL = 1024
BQ = 128
SPAN = BQ + 2 * WINDOW
TILES = SPAN // 128
STRIP = 16
NORM_ROWS = 512
PROJ_ROWS = 512
HIDDEN = -1e30
CHUNKS = 2

VMEM = pl.BlockSpec(memory_space=pltpu.VMEM)
HBM = pl.BlockSpec(memory_space=pltpu.HBM)
BF16 = jnp.bfloat16
F32 = jnp.float32


def sds(shape, dtype):
    return jax.ShapeDtypeStruct(shape, dtype)


def dot(a, b):
    return jnp.dot(a, b, preferred_element_type=F32)


def call(kernel, outs, *args, in_specs=None, out_specs=None, scratch=(), limit=24, flops=0, name=None):
    cost = pl.CostEstimate(flops=flops, bytes_accessed=4 << 20, transcendentals=0)
    return pl.pallas_call(
        kernel,
        out_shape=outs,
        in_specs=in_specs or [VMEM] * len(args),
        out_specs=out_specs or jax.tree.map(lambda _: VMEM, outs),
        scratch_shapes=scratch,
        compiler_params=pltpu.CompilerParams(vmem_limit_bytes=limit << 20),
        cost_estimate=cost,
        name=name,
    )(*args)


def rms(x, gain):
    return x * lax.rsqrt(jnp.mean(x * x, axis=-1, keepdims=True) + 1e-05) * gain


def head_ones(width):
    row = lax.broadcasted_iota(jnp.int32, (width, width), 0) // HEAD_DIM
    lane = lax.broadcasted_iota(jnp.int32, (width, width), 1) // HEAD_DIM
    return jnp.where(row == lane, 1.0 / HEAD_DIM, 0.0).astype(BF16)


def unit(x, ones):
    square = x * x
    high = square.astype(BF16)
    low = (square - high.astype(F32)).astype(BF16)
    mean = dot(high, ones) + dot(low, ones)
    return x * lax.rsqrt(mean + 1e-06)


def copy_in(pairs, sems):
    copies = [pltpu.make_async_copy(src, dst, sems.at[i]) for i, (src, dst) in enumerate(pairs)]
    for copy in copies:
        copy.start()
    return copies


def norm_kernel(
    tok_ref, gain_ref, coarse_gain_ref, normed_ref, first_ref, second_ref, buf, gains, sems
):
    rows = tok_ref.shape[0]
    count = rows // NORM_ROWS
    parts = [pl.ds(c * NORM_ROWS, NORM_ROWS) for c in range(count)]
    copies = copy_in(
        [(gain_ref, gains.at[0]), (coarse_gain_ref, gains.at[1])]
        + [(tok_ref.at[part], buf.at[part]) for part in parts],
        sems,
    )
    copies[0].wait()
    copies[1].wait()
    gain = gains[0]
    ones = jnp.ones((8, NORM_ROWS), BF16)
    pooled = []
    for c, part in enumerate(parts):
        copies[2 + c].wait()
        normed = rms(buf[part, :].astype(F32), gain).astype(BF16)
        normed_ref[part, :] = normed
        total = dot(ones, normed)[:1]
        if c * NORM_ROWS % POOL:
            pooled[-1] = pooled[-1] + total
        else:
            pooled.append(total)
    pooled = jnp.concatenate(pooled, 0) * (1.0 / POOL)
    half = WINDOW // 2
    side = lax.axis_index("head") * half
    last = (lax.axis_index("seq") % 2 == 0).astype(jnp.int32) * (rows - WINDOW)
    for ref, start in ((first_ref, last), (second_ref, rows - WINDOW - last)):
        ref[:half, :] = normed_ref[pl.ds(pl.multiple_of(start + side, half), half), :]
    first_ref[half : half + rows // POOL, :] = rms(pooled, gains[1]).astype(BF16)


def unit_columns(x):
    split = x.reshape(-1, HEAD_DIM, x.shape[1])
    mean = jnp.mean(split * split, axis=1, keepdims=True)
    return (split * lax.rsqrt(mean + 1e-06)).reshape(x.shape)


def project_columns(weight, rows):
    return lax.dot_general(weight, rows, (((0,), (1,)), ((), ())), preferred_element_type=F32)


def attention_kernel(
    base,
    q_ref,
    main_k_ref,
    main_v_ref,
    halo_k_ref,
    halo_v_ref,
    coarse_ref,
    wk_ref,
    wv_ref,
    o_ref,
    s_ref,
    p_ref,
    far_k_ref,
    far_v_ref,
    k_ref,
    v_ref,
):
    blocks = o_ref.shape[0] // BQ
    chunk = o_ref.shape[0]
    width, rows = q_ref.shape
    heads = width // HEAD_DIM
    stack = heads * BQ
    far_count = coarse_ref.shape[0]
    far_width = far_v_ref.shape[0]
    far_tiles = far_width // 128
    tiles = TILES + far_tiles
    all_blocks = rows // BQ
    lane_head = lax.broadcasted_iota(jnp.int32, (BQ, width), 1) // HEAD_DIM
    seq_index = lax.axis_index("seq")
    is_first = seq_index == 0
    is_last = seq_index == lax.axis_size("seq") - 1

    coarse = coarse_ref[...]
    far_keys = unit(dot(coarse, wk_ref[...]), head_ones(width))
    far_v_ref[...] = jnp.zeros_like(far_v_ref)
    far_v_ref[:far_count, :] = far_keys.astype(BF16)
    far_k_ref[...] = far_v_ref[...].T
    far_v_ref[:far_count, :] = dot(coarse, wv_ref[...]).astype(BF16)

    low, high = base - WINDOW, base + chunk + WINDOW
    at, start, stop = 0, low, high
    if low < 0:
        k_ref[:, :WINDOW] = halo_k_ref[:, :WINDOW]
        v_ref[:WINDOW, :] = halo_v_ref[:WINDOW, :]
        at, start = WINDOW, 0
    if high > rows:
        k_ref[:, chunk + WINDOW :] = halo_k_ref[:, WINDOW:]
        v_ref[chunk + WINDOW :, :] = halo_v_ref[WINDOW:, :]
        stop = rows
    k_ref[:, at : at + stop - start] = main_k_ref[:, start:stop]
    v_ref[at : at + stop - start, :] = main_v_ref[start:stop, :]

    def rows_at(b, size):
        return pl.ds(pl.multiple_of(b * BQ, BQ), size)

    def scores(b, slot):
        q = q_ref[:, pl.ds(pl.multiple_of(base + b * BQ, BQ), BQ)].T
        queries = jnp.concatenate(
            [jnp.where(lane_head == h, q, jnp.zeros_like(q)) for h in range(heads)], 0
        )
        keys = jnp.concatenate([k_ref[:, rows_at(b, SPAN)], far_k_ref[...]], 1)
        s_ref[slot] = dot(queries, keys)

    def hide_outside(b, slot):
        block = base // BQ + b
        for edge, distance, near, outer in (
            (is_first, block, 1, 0),
            (is_last, all_blocks - 1 - block, TILES - 2, TILES - 1),
        ):
            for tile, reach in ((near, 1), (outer, 2)):

                @pl.when(edge & (distance < reach))
                def _():
                    s_ref[slot, :, tile * 128 : tile * 128 + 128] = jnp.full(
                        (stack, 128), HIDDEN, F32
                    )

    def softmax(slot):
        lane = lax.broadcasted_iota(jnp.int32, (STRIP, 128), 1)
        ahead = lane - lax.broadcasted_iota(jnp.int32, (STRIP, 128), 0)
        for r in range(0, stack, STRIP):
            at = r % BQ
            part = [s_ref[slot, r : r + STRIP, 128 * t : 128 * t + 128] for t in range(tiles)]
            part[0] = jnp.where(ahead >= at, part[0], HIDDEN)
            part[TILES - 1] = jnp.where(ahead <= at, part[TILES - 1], HIDDEN)
            if far_count < far_width:
                used = far_count - (far_tiles - 1) * 128
                part[-1] = jnp.where(lane < used, part[-1], HIDDEN)
            peak = jnp.max(functools.reduce(jnp.maximum, part), axis=1, keepdims=True)
            part = [jnp.exp(x - peak) for x in part]
            total = jnp.sum(functools.reduce(jnp.add, part), axis=1, keepdims=True)
            scale = 1.0 / total
            for t in range(tiles):
                p_ref[slot, r : r + STRIP, 128 * t : 128 * t + 128] = (part[t] * scale).astype(BF16)

    def mix(b, slot):
        values = jnp.concatenate([v_ref[rows_at(b, SPAN), :], far_v_ref[...]], 0)
        mixed = dot(p_ref[slot], values)
        out = mixed[:BQ]
        for h in range(1, heads):
            out = jnp.where(lane_head == h, mixed[h * BQ : (h + 1) * BQ], out)
        o_ref[pl.ds(pl.multiple_of(b * BQ, BQ), BQ), :] = out.astype(BF16)

    scores(0, 0)

    @pl.loop(0, blocks // 2)
    def _(i):
        for slot in range(2):
            b = 2 * i + slot
            hide_outside(b, slot)
            mix(jnp.maximum(b - 1, 0), 1 - slot)
            scores(jnp.minimum(b + 1, blocks - 1), 1 - slot)
            softmax(slot)

    mix(blocks - 1, 1)


def out_kernel(first, own_ref, other_ref, w_ref, *rest):
    o_ref, buf, sems = rest[-3:]
    core = lax.axis_index("head")
    width = own_ref.shape[1]

    def weight(rows_of):
        rows = pl.ds(pl.multiple_of(rows_of * width, width), width)
        return w_ref[rows, pl.ds(pl.multiple_of(core * width, width), width)]

    own_w, other_w = weight(core), weight(1 - core)
    copies = []
    for c in range(own_ref.shape[0] // PROJ_ROWS):
        part = pl.ds(c * PROJ_ROWS, PROJ_ROWS)
        out = dot(own_ref[part, :], own_w) + dot(other_ref[part, :], other_w)
        buf[part, :] = out.astype(BF16)
        target = o_ref.at[pl.ds(first + c * PROJ_ROWS, PROJ_ROWS)]
        copies.append(pltpu.make_async_copy(buf.at[part], target, sems.at[c]))
        copies[-1].start()
    for copy in copies:
        copy.wait()


def swap_heads(x):
    return lax.ppermute(x, "head", [(0, 1), (1, 0)])


def swap_pairs(x, start, seq_size):
    pairs = [(i, i + 1) for i in range(start, seq_size - 1, 2)]
    return lax.ppermute(x, "seq", pairs + [(b, a) for a, b in pairs])


def body(tokens, norm_gain, coarse_gain, w_query, w_key, w_value, w_out, score_scale):
    rows, full = tokens.shape
    heads = score_scale.shape[0]
    width = heads * HEAD_DIM
    seq_size = lax.axis_size("seq")
    half = WINDOW // 2
    pooled = rows // POOL
    packet = half + -(-pooled // 16) * 16

    normed, first, second = call(
        norm_kernel,
        (sds((rows, full), BF16), sds((packet, full), BF16), sds((half, full), BF16)),
        pltpu.with_memory_space_constraint(tokens, pltpu.HBM),
        pltpu.with_memory_space_constraint(norm_gain[None], pltpu.HBM),
        pltpu.with_memory_space_constraint(coarse_gain[None], pltpu.HBM),
        in_specs=[HBM] * 3,
        scratch=[
            pltpu.VMEM((rows, full), BF16),
            pltpu.VMEM((2, 1, full), F32),
            pltpu.SemaphoreType.DMA((rows // NORM_ROWS + 2,)),
        ],
        limit=24,
        flops=2 << 30,
        name="norm",
    )
    first_in = swap_pairs(first, 0, seq_size)
    second_in = swap_pairs(second, 1, seq_size)
    factor = jnp.repeat(score_scale * HEAD_DIM ** (-0.5), HEAD_DIM)[:, None]
    queries = dot(normed, w_value).astype(BF16)
    power = seq_size & (seq_size - 1) == 0
    coarse = first[half : half + pooled]
    first_in, queries = lax.optimization_barrier((first_in, queries))
    if power:
        coarse = jnp.concatenate([coarse, first_in[half : half + pooled]], 0)
    else:
        coarse = lax.all_gather(coarse, "seq", axis=0, tiled=True)
    step = 2
    covers = 0
    covered = []
    while covers < 2 or (power and step < seq_size):
        received = None
        if power and step < seq_size:
            pairs = [(i, i ^ step) for i in range(seq_size)]
            received = lax.ppermute(coarse, "seq", pairs)
        if covers < 2:
            normed, coarse = lax.optimization_barrier((normed, coarse))
            if covers == 0:
                result = unit_columns(project_columns(w_key, normed)).astype(BF16)
            else:
                result = (unit_columns(project_columns(w_query, normed)) * factor).astype(BF16)
            if received is not None:
                received, result = lax.optimization_barrier((received, result))
            covered.append(result)
        if covers == 0:
            mine = jnp.concatenate([first_in[:half], second_in], 0)
            other = swap_heads(mine)
        if received is not None:
            coarse = jnp.concatenate([coarse, received], 0)
        covers += 1
        step *= 2
    queries, keys, values = covered[1], covered[0], queries
    core = lax.axis_index("head")
    ordered = jnp.where(core == 0, jnp.stack([mine, other]), jnp.stack([other, mine]))
    ordered = ordered.reshape(2, 2, half, full)
    odd = lax.axis_index("seq") % 2 == 1
    from_first, from_second = ordered[:, 0], ordered[:, 1]
    halo = jnp.concatenate(
        [
            jnp.where(odd, from_first, from_second).reshape(WINDOW, full),
            jnp.where(odd, from_second, from_first).reshape(WINDOW, full),
        ],
        0,
    )
    halo_keys = unit_columns(project_columns(w_key, halo)).astype(BF16)
    halo_values = dot(halo, w_value).astype(BF16)
    far_width = -(-coarse.shape[0] // 128) * 128
    chunk = rows // CHUNKS
    stack = heads * BQ
    out = []
    for c in range(CHUNKS):
        attended = call(
            functools.partial(attention_kernel, c * chunk),
            sds((chunk, width), BF16),
            queries,
            keys,
            values,
            halo_keys,
            halo_values,
            coarse,
            w_key,
            w_value,
            scratch=[
                pltpu.VMEM((2, stack, SPAN + far_width), F32),
                pltpu.VMEM((2, stack, SPAN + far_width), BF16),
                pltpu.VMEM((width, far_width), BF16),
                pltpu.VMEM((far_width, width), BF16),
                pltpu.VMEM((width, chunk + 2 * WINDOW), BF16),
                pltpu.VMEM((chunk + 2 * WINDOW, width), BF16),
            ],
            flops=10 << 30,
            name="attention",
        )
        swapped = swap_heads(attended)
        out = [
            pl.pallas_call(
                functools.partial(out_kernel, c * chunk),
                out_shape=sds((rows, width), BF16),
                in_specs=[VMEM] * 3 + [HBM] * len(out),
                out_specs=HBM,
                scratch_shapes=[
                    pltpu.VMEM((chunk, width), BF16),
                    pltpu.SemaphoreType.DMA((chunk // PROJ_ROWS,)),
                ],
                input_output_aliases={3: 0} if out else {},
                compiler_params=pltpu.CompilerParams(vmem_limit_bytes=16 << 20),
                cost_estimate=pl.CostEstimate(
                    flops=1 << 30, bytes_accessed=4 << 20, transcendentals=0
                ),
                name="out",
            )(attended, swapped, w_out, *out)
        ]
    return out[0]


def solution(mesh):
    return jax.shard_map(
        body,
        mesh=mesh,
        in_specs=(
            P(("fields", "seq"), None),
            P(),
            P(),
            P(None, "head"),
            P(None, "head"),
            P(None, "head"),
            P(),
            P("head"),
        ),
        out_specs=P(("fields", "seq"), "head"),
        check_vma=False,
    )
```

```python
import functools

import jax
import jax.numpy as jnp
from jax import lax
from jax.experimental import pallas as pl
from jax.experimental.pallas import tpu as pltpu
from jax.sharding import PartitionSpec as P

HEAD_DIM = 64
WINDOW = 256
POOL = 1024
BQ = 128
SPAN = BQ + 2 * WINDOW
TILES = SPAN // 128
STRIP = 16
NORM_ROWS = 512
PROJ_ROWS = 512
HIDDEN = -1e30

VMEM = pl.BlockSpec(memory_space=pltpu.VMEM)
HBM = pl.BlockSpec(memory_space=pltpu.HBM)
SMEM = pl.BlockSpec(memory_space=pltpu.SMEM)
BF16 = jnp.bfloat16
F32 = jnp.float32


def sds(shape, dtype):
    return jax.ShapeDtypeStruct(shape, dtype)


def dot(a, b):
    return jnp.dot(a, b, preferred_element_type=F32)


def call(kernel, outs, *args, in_specs=None, out_specs=None, scratch=(), limit=24, flops=0, name=None):
    cost = pl.CostEstimate(flops=flops, bytes_accessed=4 << 20, transcendentals=0)
    return pl.pallas_call(
        kernel,
        out_shape=outs,
        in_specs=in_specs or [VMEM] * len(args),
        out_specs=out_specs or jax.tree.map(lambda _: VMEM, outs),
        scratch_shapes=scratch,
        compiler_params=pltpu.CompilerParams(vmem_limit_bytes=limit << 20),
        cost_estimate=cost,
        name=name,
    )(*args)


def rms(x, gain):
    return x * lax.rsqrt(jnp.mean(x * x, axis=-1, keepdims=True) + 1e-05) * gain


def head_ones(width):
    row = lax.broadcasted_iota(jnp.int32, (width, width), 0) // HEAD_DIM
    lane = lax.broadcasted_iota(jnp.int32, (width, width), 1) // HEAD_DIM
    return jnp.where(row == lane, 1.0 / HEAD_DIM, 0.0).astype(BF16)


def unit(x, ones):
    square = x * x
    high = square.astype(BF16)
    low = (square - high.astype(F32)).astype(BF16)
    mean = dot(high, ones) + dot(low, ones)
    return x * lax.rsqrt(mean + 1e-06)


def copy_in(pairs, sems):
    copies = [pltpu.make_async_copy(src, dst, sems.at[i]) for i, (src, dst) in enumerate(pairs)]
    for copy in copies:
        copy.start()
    return copies


def norm_kernel(
    tok_ref,
    gain_ref,
    coarse_gain_ref,
    normed_ref,
    coarse_ref,
    first_ref,
    second_ref,
    buf,
    gains,
    sems,
):
    rows = tok_ref.shape[0]
    count = rows // NORM_ROWS
    parts = [pl.ds(c * NORM_ROWS, NORM_ROWS) for c in range(count)]
    copies = copy_in(
        [(gain_ref, gains.at[0]), (coarse_gain_ref, gains.at[1])]
        + [(tok_ref.at[part], buf.at[part]) for part in parts],
        sems,
    )
    copies[0].wait()
    copies[1].wait()
    gain = gains[0]
    ones = jnp.ones((8, NORM_ROWS), BF16)
    pooled = []
    for c, part in enumerate(parts):
        copies[2 + c].wait()
        normed = rms(buf[part, :].astype(F32), gain).astype(BF16)
        normed_ref[part, :] = normed
        total = dot(ones, normed)[:1]
        if c * NORM_ROWS % POOL:
            pooled[-1] = pooled[-1] + total
        else:
            pooled.append(total)
    pooled = jnp.concatenate(pooled, 0) * (1.0 / POOL)
    last = jnp.where(lax.axis_index("seq") % 2 == 0, rows - WINDOW, 0)
    for ref, start in ((first_ref, last), (second_ref, rows - WINDOW - last)):
        ref[...] = normed_ref[pl.ds(pl.multiple_of(start, WINDOW), WINDOW), :]
    coarse_ref[...] = rms(pooled, gains[1]).astype(BF16)


def unit_columns(x):
    split = x.reshape(-1, HEAD_DIM, x.shape[1])
    mean = jnp.mean(split * split, axis=1, keepdims=True)
    return split * lax.rsqrt(mean + 1e-06)


def project_columns(weight, rows):
    return lax.dot_general(weight, rows, (((0,), (1,)), ((), ())), preferred_element_type=F32)


def row_parts(rows):
    return [pl.ds(start, PROJ_ROWS) for start in range(0, rows, PROJ_ROWS)]


def query_part(normed, w_ref, scale_ref, q_ref, part):
    q = unit_columns(project_columns(w_ref[...], normed))
    for h in range(q.shape[0]):
        factor = scale_ref[h] * HEAD_DIM ** (-0.5)
        q_ref[h * HEAD_DIM : (h + 1) * HEAD_DIM, part] = (q[h] * factor).astype(BF16)


def query_kernel(normed_ref, w_ref, scale_ref, q_ref):
    for part in row_parts(normed_ref.shape[0]):
        query_part(normed_ref[part, :], w_ref, scale_ref, q_ref, part)


def key_value_kernel(normed_ref, wk_ref, wv_ref, k_ref, v_ref):
    for part in row_parts(normed_ref.shape[0]):
        normed = normed_ref[part, :]
        k = unit_columns(project_columns(wk_ref[...], normed))
        k_ref[:, part] = k.reshape(k_ref.shape[0], PROJ_ROWS).astype(BF16)
        v_ref[part, :] = dot(normed, wv_ref[...]).astype(BF16)


def all_kernel(normed_ref, wk_ref, wv_ref, wq_ref, scale_ref, k_ref, v_ref, q_ref):
    key_value_kernel(normed_ref, wk_ref, wv_ref, k_ref, v_ref)
    query_kernel(normed_ref, wq_ref, scale_ref, q_ref)


def halo_kernel(first_ref, second_ref, wk_ref, wv_ref, k_ref, v_ref):
    odd = lax.axis_index("seq") % 2
    for ref, start in ((first_ref, (1 - odd) * WINDOW), (second_ref, odd * WINDOW)):
        part = pl.ds(pl.multiple_of(start, WINDOW), WINDOW)
        keys = unit_columns(project_columns(wk_ref[...], ref[...]))
        k_ref[:, part] = keys.reshape(k_ref.shape[0], WINDOW).astype(BF16)
        v_ref[part, :] = dot(ref[...], wv_ref[...]).astype(BF16)


def far_kernel(coarse_ref, wk_ref, wv_ref, k_ref, v_ref):
    count = coarse_ref.shape[0]
    coarse = coarse_ref[...]
    keys = unit(dot(coarse, wk_ref[...]), head_ones(v_ref.shape[1]))
    v_ref[...] = jnp.zeros_like(v_ref)
    v_ref[:count, :] = keys.astype(BF16)
    k_ref[...] = v_ref[...].T
    v_ref[:count, :] = dot(coarse, wv_ref[...]).astype(BF16)


def attention_kernel(far_count, edges, q_ref, main_k_ref, main_v_ref, *rest):
    if edges:
        halo_k_ref, halo_v_ref, *rest = rest
    far_k_ref, far_v_ref, o_ref, s_ref, p_ref, *rest = rest
    chunk = o_ref.shape[0]
    blocks = chunk // BQ
    width, rows = q_ref.shape
    heads = width // HEAD_DIM
    stack = heads * BQ
    far_width = far_v_ref.shape[0]
    far_tiles = far_width // 128
    tiles = TILES + far_tiles
    lane_head = lax.broadcasted_iota(jnp.int32, (BQ, width), 1) // HEAD_DIM
    seq_index = lax.axis_index("seq")
    is_first = seq_index == 0
    is_last = seq_index == lax.axis_size("seq") - 1
    quarter = chunk // 2

    if edges:
        k_ref, v_ref = rest
        inner = quarter + WINDOW
        k_ref[:, :WINDOW] = halo_k_ref[:, :WINDOW]
        v_ref[:WINDOW, :] = halo_v_ref[:WINDOW, :]
        k_ref[:, WINDOW : WINDOW + inner] = main_k_ref[:, :inner]
        v_ref[WINDOW : WINDOW + inner, :] = main_v_ref[:inner, :]
        k_ref[:, WINDOW + inner : WINDOW + 2 * inner] = main_k_ref[:, rows - inner :]
        v_ref[WINDOW + inner : WINDOW + 2 * inner, :] = main_v_ref[rows - inner :, :]
        k_ref[:, WINDOW + 2 * inner :] = halo_k_ref[:, WINDOW:]
        v_ref[WINDOW + 2 * inner :, :] = halo_v_ref[WINDOW:, :]
    else:
        k_ref, v_ref = main_k_ref, main_v_ref

    def at_second(b):
        return jnp.where(b >= blocks // 2, 1, 0)

    def query_rows(b):
        start = b * BQ + at_second(b) * (rows - chunk) if edges else quarter + b * BQ
        return pl.ds(pl.multiple_of(start, BQ), BQ)

    def key_rows(b):
        start = b * BQ + at_second(b) * 2 * WINDOW if edges else quarter - WINDOW + b * BQ
        return pl.ds(pl.multiple_of(start, BQ), SPAN)

    def scores(b, slot):
        q = q_ref[:, query_rows(b)].T
        queries = jnp.concatenate(
            [jnp.where(lane_head == h, q, jnp.zeros_like(q)) for h in range(heads)], 0
        )
        keys = jnp.concatenate([k_ref[:, key_rows(b)], far_k_ref[...]], 1)
        s_ref[slot] = dot(queries, keys)

    def hide_outside(b, slot):
        for edge, distance, near, outer in (
            (is_first, b, 1, 0),
            (is_last, blocks - 1 - b, TILES - 2, TILES - 1),
        ):
            for tile, reach in ((near, 1), (outer, 2)):

                @pl.when(edge & (distance < reach))
                def _():
                    s_ref[slot, :, tile * 128 : tile * 128 + 128] = jnp.full(
                        (stack, 128), HIDDEN, F32
                    )

    def softmax(slot):
        lane = lax.broadcasted_iota(jnp.int32, (STRIP, 128), 1)
        ahead = lane - lax.broadcasted_iota(jnp.int32, (STRIP, 128), 0)
        for r in range(0, stack, STRIP):
            at = r % BQ
            part = [s_ref[slot, r : r + STRIP, 128 * t : 128 * t + 128] for t in range(tiles)]
            part[0] = jnp.where(ahead >= at, part[0], HIDDEN)
            part[TILES - 1] = jnp.where(ahead <= at, part[TILES - 1], HIDDEN)
            if far_count < far_width:
                used = far_count - (far_tiles - 1) * 128
                part[-1] = jnp.where(lane < used, part[-1], HIDDEN)
            peak = jnp.max(functools.reduce(jnp.maximum, part), axis=1, keepdims=True)
            part = [jnp.exp(x - peak) for x in part]
            total = jnp.sum(functools.reduce(jnp.add, part), axis=1, keepdims=True)
            scale = 1.0 / total
            for t in range(tiles):
                p_ref[slot, r : r + STRIP, 128 * t : 128 * t + 128] = (part[t] * scale).astype(BF16)

    def mix(b, slot):
        values = jnp.concatenate([v_ref[key_rows(b), :], far_v_ref[...]], 0)
        mixed = dot(p_ref[slot], values)
        out = mixed[:BQ]
        for h in range(1, heads):
            out = jnp.where(lane_head == h, mixed[h * BQ : (h + 1) * BQ], out)
        o_ref[pl.ds(pl.multiple_of(b * BQ, BQ), BQ), :] = out.astype(BF16)

    scores(0, 0)

    @pl.loop(0, blocks // 2)
    def _(i):
        for slot in range(2):
            b = 2 * i + slot
            if edges:
                hide_outside(b, slot)
            mix(jnp.maximum(b - 1, 0), 1 - slot)
            scores(jnp.minimum(b + 1, blocks - 1), 1 - slot)
            softmax(slot)

    mix(blocks - 1, 1)


def out_kernel(starts, own_ref, other_ref, w_ref, *rest):
    o_ref, buf, sems = rest[-3:]
    core = lax.axis_index("head")
    width = own_ref.shape[1]

    def weight(rows_of):
        rows = pl.ds(pl.multiple_of(rows_of * width, width), width)
        return w_ref[rows, pl.ds(pl.multiple_of(core * width, width), width)]

    own_w, other_w = weight(core), weight(1 - core)
    copies = []
    for c in range(own_ref.shape[0] // PROJ_ROWS):
        part = pl.ds(c * PROJ_ROWS, PROJ_ROWS)
        out = dot(own_ref[part, :], own_w) + dot(other_ref[part, :], other_w)
        buf[part, :] = out.astype(BF16)
        target = o_ref.at[pl.ds(starts[c], PROJ_ROWS)]
        copies.append(pltpu.make_async_copy(buf.at[part], target, sems.at[c]))
        copies[-1].start()
    for copy in copies:
        copy.wait()


def swap_heads(x):
    return lax.ppermute(x, "head", [(0, 1), (1, 0)])


def swap_pairs(x, start, seq_size):
    pairs = [(i, i + 1) for i in range(start, seq_size - 1, 2)]
    return lax.ppermute(x, "seq", pairs + [(b, a) for a, b in pairs])


def body(tokens, norm_gain, coarse_gain, w_query, w_key, w_value, w_out, score_scale):
    rows, full = tokens.shape
    heads = score_scale.shape[0]
    width = heads * HEAD_DIM
    seq_size = lax.axis_size("seq")
    pooled = rows // POOL
    power = seq_size & (seq_size - 1) == 0

    normed, coarse, first, second = call(
        norm_kernel,
        (
            sds((rows, full), BF16),
            sds((pooled, full), BF16),
            sds((WINDOW, full), BF16),
            sds((WINDOW, full), BF16),
        ),
        pltpu.with_memory_space_constraint(tokens, pltpu.HBM),
        pltpu.with_memory_space_constraint(norm_gain[None], pltpu.HBM),
        pltpu.with_memory_space_constraint(coarse_gain[None], pltpu.HBM),
        in_specs=[HBM] * 3,
        scratch=[
            pltpu.VMEM((rows, full), BF16),
            pltpu.VMEM((2, 1, full), F32),
            pltpu.SemaphoreType.DMA((rows // NORM_ROWS + 2,)),
        ],
        flops=2 << 30,
        name="norm",
    )
    columns = sds((width, rows), BF16)
    project = functools.partial(call, flops=4 << 30)

    def keys_values_of(x):
        outs = (columns, sds((rows, width), BF16))
        return project(key_value_kernel, outs, x, w_key, w_value, name="keys_values")

    def all_of(x):
        outs = (columns, sds((rows, width), BF16), columns)
        specs = [VMEM] * 4 + [SMEM]
        return project(
            all_kernel, outs, x, w_key, w_value, w_query, score_scale, in_specs=specs, name="all"
        )

    def queries_of(x):
        specs = [VMEM, VMEM, SMEM]
        return project(
            query_kernel, columns, x, w_query, score_scale, in_specs=specs, name="queries"
        )

    first_in = second_in = None
    pending = [keys_values_of, queries_of]
    covered = []
    step = 1
    while pending or (power and step < seq_size):
        received = None
        if power and step < seq_size:
            pairs = [(i, i ^ step) for i in range(seq_size)]
            received = lax.ppermute(coarse, "seq", pairs)
        if pending:
            normed, coarse = lax.optimization_barrier((normed, coarse))
            result = pending.pop(0)(normed)
            if received is not None:
                received, result = lax.optimization_barrier((received, result))
            covered.append(result)
        if first_in is None:
            first_in = swap_pairs(first, 0, seq_size)
        if received is not None:
            coarse = jnp.concatenate([coarse, received], 0)
        if second_in is None and step > 1:
            second, coarse = lax.optimization_barrier((second, coarse))
            second_in = swap_pairs(second, 1, seq_size)
        step *= 2
    (keys, values), queries = covered
    if not power:
        coarse = lax.all_gather(coarse, "seq", axis=0, tiled=True)
    far_count = coarse.shape[0]
    far_width = -(-far_count // 128) * 128
    far_keys, far_values = call(
        far_kernel,
        (sds((width, far_width), BF16), sds((far_width, width), BF16)),
        coarse,
        w_key,
        w_value,
        limit=16,
        name="far",
    )
    stack = heads * BQ
    chunk = rows // 2
    scratch = [
        pltpu.VMEM((2, stack, SPAN + far_width), F32),
        pltpu.VMEM((2, stack, SPAN + far_width), BF16),
    ]
    attend = functools.partial(call, flops=10 << 30)
    middle = attend(
        functools.partial(attention_kernel, far_count, False),
        sds((chunk, width), BF16),
        queries,
        keys,
        values,
        far_keys,
        far_values,
        scratch=scratch,
        name="middle",
    )
    middle_in = swap_heads(middle)
    first_in, second_in, middle = lax.optimization_barrier((first_in, second_in, middle))
    halo_keys, halo_values = call(
        halo_kernel,
        (sds((width, 2 * WINDOW), BF16), sds((2 * WINDOW, width), BF16)),
        first_in,
        second_in,
        w_key,
        w_value,
        limit=16,
        name="halo",
    )
    outer = attend(
        functools.partial(attention_kernel, far_count, True),
        sds((chunk, width), BF16),
        queries,
        keys,
        values,
        halo_keys,
        halo_values,
        far_keys,
        far_values,
        scratch=scratch
        + [
            pltpu.VMEM((width, chunk + 4 * WINDOW), BF16),
            pltpu.VMEM((chunk + 4 * WINDOW, width), BF16),
        ],
        name="outer",
    )
    outer_in = swap_heads(outer)
    quarter = rows // 4
    spans = [
        (middle, middle_in, range(quarter, rows - quarter, PROJ_ROWS)),
        (
            outer,
            outer_in,
            [*range(0, quarter, PROJ_ROWS), *range(rows - quarter, rows, PROJ_ROWS)],
        ),
    ]
    out = []
    for attended, swapped, starts in spans:
        out = [
            pl.pallas_call(
                functools.partial(out_kernel, list(starts)),
                out_shape=sds((rows, width), BF16),
                in_specs=[VMEM] * 3 + [HBM] * len(out),
                out_specs=HBM,
                scratch_shapes=[
                    pltpu.VMEM((chunk, width), BF16),
                    pltpu.SemaphoreType.DMA((chunk // PROJ_ROWS,)),
                ],
                input_output_aliases={3: 0} if out else {},
                compiler_params=pltpu.CompilerParams(vmem_limit_bytes=16 << 20),
                cost_estimate=pl.CostEstimate(
                    flops=1 << 30, bytes_accessed=4 << 20, transcendentals=0
                ),
                name="out",
            )(attended, swapped, w_out, *out)
        ]
    return out[0]


def solution(mesh):
    return jax.shard_map(
        body,
        mesh=mesh,
        in_specs=(
            P(("fields", "seq"), None),
            P(),
            P(),
            P(None, "head"),
            P(None, "head"),
            P(None, "head"),
            P(),
            P("head"),
        ),
        out_specs=P(("fields", "seq"), "head"),
        check_vma=False,
    )
```

```python
import functools

import jax
import jax.numpy as jnp
from jax import lax
from jax.experimental import pallas as pl
from jax.experimental.pallas import tpu as pltpu
from jax.sharding import PartitionSpec as P

HEAD_DIM = 64
WINDOW = 256
POOL = 1024
BQ = 128
SPAN = BQ + 2 * WINDOW
TILES = SPAN // 128
STRIP = 16
NORM_ROWS = 512
PROJ_ROWS = 512
EDGE_ROWS = 512
OUT_ROWS = 512
HIDDEN = -1e30

VMEM = pl.BlockSpec(memory_space=pltpu.VMEM)
HBM = pl.BlockSpec(memory_space=pltpu.HBM)
SMEM = pl.BlockSpec(memory_space=pltpu.SMEM)
BF16 = jnp.bfloat16
F32 = jnp.float32


def sds(shape, dtype):
    return jax.ShapeDtypeStruct(shape, dtype)


def dot(a, b):
    return jnp.dot(a, b, preferred_element_type=F32)


def call(kernel, outs, *args, in_specs=None, out_specs=None, scratch=(), limit=24, flops=0, name=None):
    cost = pl.CostEstimate(flops=flops, bytes_accessed=4 << 20, transcendentals=0)
    return pl.pallas_call(
        kernel,
        out_shape=outs,
        in_specs=in_specs or [VMEM] * len(args),
        out_specs=out_specs or jax.tree.map(lambda _: VMEM, outs),
        scratch_shapes=scratch,
        compiler_params=pltpu.CompilerParams(vmem_limit_bytes=limit << 20),
        cost_estimate=cost,
        name=name,
    )(*args)


def rms(x, gain):
    return x * lax.rsqrt(jnp.mean(x * x, axis=-1, keepdims=True) + 1e-05) * gain


def head_ones(width):
    row = lax.broadcasted_iota(jnp.int32, (width, width), 0) // HEAD_DIM
    lane = lax.broadcasted_iota(jnp.int32, (width, width), 1) // HEAD_DIM
    return jnp.where(row == lane, 1.0 / HEAD_DIM, 0.0).astype(BF16)


def unit(x, ones):
    square = x * x
    high = square.astype(BF16)
    low = (square - high.astype(F32)).astype(BF16)
    mean = dot(high, ones) + dot(low, ones)
    return x * lax.rsqrt(mean + 1e-06)


def copy_in(pairs, sems):
    copies = [pltpu.make_async_copy(src, dst, sems.at[i]) for i, (src, dst) in enumerate(pairs)]
    for copy in copies:
        copy.start()
    return copies


def norm_kernel(
    tok_ref,
    gain_ref,
    coarse_gain_ref,
    normed_ref,
    coarse_ref,
    first_ref,
    second_ref,
    buf,
    gains,
    sems,
):
    rows = tok_ref.shape[0]
    count = rows // NORM_ROWS
    parts = [pl.ds(c * NORM_ROWS, NORM_ROWS) for c in range(count)]
    copies = copy_in(
        [(gain_ref, gains.at[0]), (coarse_gain_ref, gains.at[1])]
        + [(tok_ref.at[part], buf.at[part]) for part in parts],
        sems,
    )
    copies[0].wait()
    copies[1].wait()
    gain = gains[0]
    ones = jnp.ones((8, NORM_ROWS), BF16)
    pooled = []
    for c, part in enumerate(parts):
        copies[2 + c].wait()
        normed = rms(buf[part, :].astype(F32), gain).astype(BF16)
        normed_ref[part, :] = normed
        total = dot(ones, normed)[:1]
        if c * NORM_ROWS % POOL:
            pooled[-1] = pooled[-1] + total
        else:
            pooled.append(total)
    pooled = jnp.concatenate(pooled, 0) * (1.0 / POOL)
    last = jnp.where(lax.axis_index("seq") % 2 == 0, rows - WINDOW, 0)
    for ref, start in ((first_ref, last), (second_ref, rows - WINDOW - last)):
        ref[...] = normed_ref[pl.ds(pl.multiple_of(start, WINDOW), WINDOW), :]
    coarse_ref[...] = rms(pooled, gains[1]).astype(BF16)


def unit_columns(x):
    split = x.reshape(-1, HEAD_DIM, x.shape[1])
    mean = jnp.mean(split * split, axis=1, keepdims=True)
    return split * lax.rsqrt(mean + 1e-06)


def project_columns(weight, rows):
    return lax.dot_general(weight, rows, (((0,), (1,)), ((), ())), preferred_element_type=F32)


def row_parts(rows):
    return [pl.ds(start, PROJ_ROWS) for start in range(0, rows, PROJ_ROWS)]


def query_part(normed, w_ref, scale_ref, q_ref, part):
    q = unit_columns(project_columns(w_ref[...], normed))
    for h in range(q.shape[0]):
        factor = scale_ref[h] * HEAD_DIM ** (-0.5)
        q_ref[h * HEAD_DIM : (h + 1) * HEAD_DIM, part] = (q[h] * factor).astype(BF16)


def query_kernel(normed_ref, w_ref, scale_ref, q_ref):
    for part in row_parts(normed_ref.shape[0]):
        query_part(normed_ref[part, :], w_ref, scale_ref, q_ref, part)


def key_value_kernel(normed_ref, wk_ref, wv_ref, k_ref, v_ref):
    for part in row_parts(normed_ref.shape[0]):
        normed = normed_ref[part, :]
        k = unit_columns(project_columns(wk_ref[...], normed))
        k_ref[:, part] = k.reshape(k_ref.shape[0], PROJ_ROWS).astype(BF16)
        v_ref[part, :] = dot(normed, wv_ref[...]).astype(BF16)


def all_kernel(normed_ref, wk_ref, wv_ref, wq_ref, scale_ref, k_ref, v_ref, q_ref):
    key_value_kernel(normed_ref, wk_ref, wv_ref, k_ref, v_ref)
    query_kernel(normed_ref, wq_ref, scale_ref, q_ref)


def halo_kernel(first_ref, second_ref, wk_ref, wv_ref, k_ref, v_ref):
    odd = lax.axis_index("seq") % 2
    for ref, start in ((first_ref, (1 - odd) * WINDOW), (second_ref, odd * WINDOW)):
        part = pl.ds(pl.multiple_of(start, WINDOW), WINDOW)
        keys = unit_columns(project_columns(wk_ref[...], ref[...]))
        k_ref[:, part] = keys.reshape(k_ref.shape[0], WINDOW).astype(BF16)
        v_ref[part, :] = dot(ref[...], wv_ref[...]).astype(BF16)


def far_kernel(coarse_ref, wk_ref, wv_ref, k_ref, v_ref):
    count = coarse_ref.shape[0]
    coarse = coarse_ref[...]
    keys = unit(dot(coarse, wk_ref[...]), head_ones(v_ref.shape[1]))
    v_ref[...] = jnp.zeros_like(v_ref)
    v_ref[:count, :] = keys.astype(BF16)
    k_ref[...] = v_ref[...].T
    v_ref[:count, :] = dot(coarse, wv_ref[...]).astype(BF16)


def attention_kernel(far_count, edges, q_ref, main_k_ref, main_v_ref, *rest):
    if edges:
        halo_k_ref, halo_v_ref, *rest = rest
    far_k_ref, far_v_ref, o_ref, s_ref, p_ref, *rest = rest
    chunk = o_ref.shape[0]
    blocks = chunk // BQ
    width, rows = q_ref.shape
    heads = width // HEAD_DIM
    stack = heads * BQ
    far_width = far_v_ref.shape[0]
    far_tiles = far_width // 128
    tiles = TILES + far_tiles
    lane_head = lax.broadcasted_iota(jnp.int32, (BQ, width), 1) // HEAD_DIM
    seq_index = lax.axis_index("seq")
    is_first = seq_index == 0
    is_last = seq_index == lax.axis_size("seq") - 1
    side = chunk // 2 if edges else (rows - chunk) // 2

    if edges:
        k_ref, v_ref = rest
        inner = side + WINDOW
        k_ref[:, :WINDOW] = halo_k_ref[:, :WINDOW]
        v_ref[:WINDOW, :] = halo_v_ref[:WINDOW, :]
        k_ref[:, WINDOW : WINDOW + inner] = main_k_ref[:, :inner]
        v_ref[WINDOW : WINDOW + inner, :] = main_v_ref[:inner, :]
        k_ref[:, WINDOW + inner : WINDOW + 2 * inner] = main_k_ref[:, rows - inner :]
        v_ref[WINDOW + inner : WINDOW + 2 * inner, :] = main_v_ref[rows - inner :, :]
        k_ref[:, WINDOW + 2 * inner :] = halo_k_ref[:, WINDOW:]
        v_ref[WINDOW + 2 * inner :, :] = halo_v_ref[WINDOW:, :]
    else:
        k_ref, v_ref = main_k_ref, main_v_ref

    def at_second(b):
        return jnp.where(b >= blocks // 2, 1, 0)

    def query_rows(b):
        start = b * BQ + at_second(b) * (rows - chunk) if edges else side + b * BQ
        return pl.ds(pl.multiple_of(start, BQ), BQ)

    def key_rows(b):
        start = b * BQ + at_second(b) * 2 * WINDOW if edges else side - WINDOW + b * BQ
        return pl.ds(pl.multiple_of(start, BQ), SPAN)

    def scores(b, slot):
        q = q_ref[:, query_rows(b)].T
        queries = jnp.concatenate(
            [jnp.where(lane_head == h, q, jnp.zeros_like(q)) for h in range(heads)], 0
        )
        keys = jnp.concatenate([k_ref[:, key_rows(b)], far_k_ref[...]], 1)
        s_ref[slot] = dot(queries, keys)

    def hide_outside(b, slot):
        for edge, distance, near, outer in (
            (is_first, b, 1, 0),
            (is_last, blocks - 1 - b, TILES - 2, TILES - 1),
        ):
            for tile, reach in ((near, 1), (outer, 2)):

                @pl.when(edge & (distance < reach))
                def _():
                    s_ref[slot, :, tile * 128 : tile * 128 + 128] = jnp.full(
                        (stack, 128), HIDDEN, F32
                    )

    def softmax(slot):
        lane = lax.broadcasted_iota(jnp.int32, (STRIP, 128), 1)
        ahead = lane - lax.broadcasted_iota(jnp.int32, (STRIP, 128), 0)
        for r in range(0, stack, STRIP):
            at = r % BQ
            part = [s_ref[slot, r : r + STRIP, 128 * t : 128 * t + 128] for t in range(tiles)]
            part[0] = jnp.where(ahead >= at, part[0], HIDDEN)
            part[TILES - 1] = jnp.where(ahead <= at, part[TILES - 1], HIDDEN)
            if far_count < far_width:
                used = far_count - (far_tiles - 1) * 128
                part[-1] = jnp.where(lane < used, part[-1], HIDDEN)
            peak = jnp.max(functools.reduce(jnp.maximum, part), axis=1, keepdims=True)
            part = [jnp.exp(x - peak) for x in part]
            total = jnp.sum(functools.reduce(jnp.add, part), axis=1, keepdims=True)
            scale = 1.0 / total
            for t in range(tiles):
                p_ref[slot, r : r + STRIP, 128 * t : 128 * t + 128] = (part[t] * scale).astype(BF16)

    def mix(b, slot):
        values = jnp.concatenate([v_ref[key_rows(b), :], far_v_ref[...]], 0)
        mixed = dot(p_ref[slot], values)
        out = mixed[:BQ]
        for h in range(1, heads):
            out = jnp.where(lane_head == h, mixed[h * BQ : (h + 1) * BQ], out)
        o_ref[pl.ds(pl.multiple_of(b * BQ, BQ), BQ), :] = out.astype(BF16)

    def step(b, slot, mixes=True, scored=True):
        if edges:
            hide_outside(b, slot)
        if mixes:
            mix(b - 1, 1 - slot)
        if scored:
            scores(b + 1, 1 - slot)
        softmax(slot)

    scores(0, 0)
    step(0, 0, mixes=False)

    @pl.loop(0, (blocks - 2) // 2)
    def _(i):
        step(2 * i + 1, 1)
        step(2 * i + 2, 0)

    step(blocks - 1, 1, scored=False)
    mix(blocks - 1, 1)


def out_kernel(starts, own_ref, other_ref, w_ref, *rest):
    o_ref, buf, sems = rest[-3:]
    core = lax.axis_index("head")
    width = own_ref.shape[1]

    def weight(rows_of):
        rows = pl.ds(pl.multiple_of(rows_of * width, width), width)
        return w_ref[rows, pl.ds(pl.multiple_of(core * width, width), width)]

    both_w = jnp.concatenate([weight(core), weight(1 - core)], 0)
    copies = []
    for c in range(own_ref.shape[0] // OUT_ROWS):
        part = pl.ds(c * OUT_ROWS, OUT_ROWS)
        out = dot(jnp.concatenate([own_ref[part, :], other_ref[part, :]], 1), both_w)
        buf[part, :] = out.astype(BF16)
        target = o_ref.at[pl.ds(starts[c], OUT_ROWS)]
        copies.append(pltpu.make_async_copy(buf.at[part], target, sems.at[c]))
        copies[-1].start()
    for copy in copies:
        copy.wait()


def swap_heads(x):
    return lax.ppermute(x, "head", [(0, 1), (1, 0)])


def swap_pairs(x, start, seq_size):
    pairs = [(i, i + 1) for i in range(start, seq_size - 1, 2)]
    return lax.ppermute(x, "seq", pairs + [(b, a) for a, b in pairs])


def body(tokens, norm_gain, coarse_gain, w_query, w_key, w_value, w_out, score_scale):
    rows, full = tokens.shape
    heads = score_scale.shape[0]
    width = heads * HEAD_DIM
    seq_size = lax.axis_size("seq")
    pooled = rows // POOL
    power = seq_size & (seq_size - 1) == 0

    normed, coarse, first, second = call(
        norm_kernel,
        (
            sds((rows, full), BF16),
            sds((pooled, full), BF16),
            sds((WINDOW, full), BF16),
            sds((WINDOW, full), BF16),
        ),
        pltpu.with_memory_space_constraint(tokens, pltpu.HBM),
        pltpu.with_memory_space_constraint(norm_gain[None], pltpu.HBM),
        pltpu.with_memory_space_constraint(coarse_gain[None], pltpu.HBM),
        in_specs=[HBM] * 3,
        scratch=[
            pltpu.VMEM((rows, full), BF16),
            pltpu.VMEM((2, 1, full), F32),
            pltpu.SemaphoreType.DMA((rows // NORM_ROWS + 2,)),
        ],
        flops=2 << 30,
        name="norm",
    )
    columns = sds((width, rows), BF16)
    project = functools.partial(call, flops=4 << 30)

    def keys_values_of(x):
        outs = (columns, sds((rows, width), BF16))
        return project(key_value_kernel, outs, x, w_key, w_value, name="keys_values")

    def all_of(x):
        outs = (columns, sds((rows, width), BF16), columns)
        specs = [VMEM] * 4 + [SMEM]
        return project(
            all_kernel, outs, x, w_key, w_value, w_query, score_scale, in_specs=specs, name="all"
        )

    def queries_of(x):
        specs = [VMEM, VMEM, SMEM]
        return project(
            query_kernel, columns, x, w_query, score_scale, in_specs=specs, name="queries"
        )

    first_in = second_in = None
    pending = [keys_values_of, queries_of]
    covered = []
    steps = [1 << i for i in reversed(range(seq_size.bit_length() - 1))] if power else []
    while pending or steps:
        received = None
        if steps:
            step = steps.pop(0)
            pairs = [(i, i ^ step) for i in range(seq_size)]
            received = lax.ppermute(coarse, "seq", pairs)
        if pending:
            normed, coarse = lax.optimization_barrier((normed, coarse))
            result = pending.pop(0)(normed)
            if received is not None:
                received, result = lax.optimization_barrier((received, result))
            covered.append(result)
        if received is not None:
            coarse = jnp.concatenate([coarse, received], 0)
        if not pending and second_in is None:
            second, coarse = lax.optimization_barrier((second, coarse))
            first_in = swap_pairs(first, 0, seq_size)
            second_in = swap_pairs(second, 1, seq_size)
    (keys, values), queries = covered
    if not power:
        coarse = lax.all_gather(coarse, "seq", axis=0, tiled=True)
    far_count = coarse.shape[0]
    far_width = -(-far_count // 128) * 128
    far_keys, far_values = call(
        far_kernel,
        (sds((width, far_width), BF16), sds((far_width, width), BF16)),
        coarse,
        w_key,
        w_value,
        limit=16,
        name="far",
    )
    stack = heads * BQ
    scratch = [
        pltpu.VMEM((2, stack, SPAN + far_width), F32),
        pltpu.VMEM((2, stack, SPAN + far_width), BF16),
    ]
    attend = functools.partial(call, flops=10 << 30)
    middle = attend(
        functools.partial(attention_kernel, far_count, False),
        sds((rows - 2 * EDGE_ROWS, width), BF16),
        queries,
        keys,
        values,
        far_keys,
        far_values,
        scratch=scratch,
        name="middle",
    )
    middle_in = swap_heads(middle)
    first_in, second_in, middle = lax.optimization_barrier((first_in, second_in, middle))
    halo_keys, halo_values = call(
        halo_kernel,
        (sds((width, 2 * WINDOW), BF16), sds((2 * WINDOW, width), BF16)),
        first_in,
        second_in,
        w_key,
        w_value,
        limit=16,
        name="halo",
    )
    outer = attend(
        functools.partial(attention_kernel, far_count, True),
        sds((2 * EDGE_ROWS, width), BF16),
        queries,
        keys,
        values,
        halo_keys,
        halo_values,
        far_keys,
        far_values,
        scratch=scratch
        + [
            pltpu.VMEM((width, 2 * EDGE_ROWS + 4 * WINDOW), BF16),
            pltpu.VMEM((2 * EDGE_ROWS + 4 * WINDOW, width), BF16),
        ],
        name="outer",
    )
    outer_in = swap_heads(outer)
    last = rows - EDGE_ROWS
    spans = [
        (middle, middle_in, [*range(EDGE_ROWS, last, OUT_ROWS)]),
        (outer, outer_in, [*range(0, EDGE_ROWS, OUT_ROWS), *range(last, rows, OUT_ROWS)]),
    ]
    out = []
    for attended, swapped, starts in spans:
        out = [
            pl.pallas_call(
                functools.partial(out_kernel, starts),
                out_shape=sds((rows, width), BF16),
                in_specs=[VMEM] * 3 + [HBM] * len(out),
                out_specs=HBM,
                scratch_shapes=[
                    pltpu.VMEM(attended.shape, BF16),
                    pltpu.SemaphoreType.DMA((len(starts),)),
                ],
                input_output_aliases={3: 0} if out else {},
                compiler_params=pltpu.CompilerParams(vmem_limit_bytes=16 << 20),
                cost_estimate=pl.CostEstimate(
                    flops=1 << 30, bytes_accessed=4 << 20, transcendentals=0
                ),
                name="out",
            )(attended, swapped, w_out, *out)
        ]
    return out[0]


def solution(mesh):
    return jax.shard_map(
        body,
        mesh=mesh,
        in_specs=(
            P(("fields", "seq"), None),
            P(),
            P(),
            P(None, "head"),
            P(None, "head"),
            P(None, "head"),
            P(),
            P("head"),
        ),
        out_specs=P(("fields", "seq"), "head"),
        check_vma=False,
    )
```

```python
import functools

import jax
import jax.numpy as jnp
from jax import lax
from jax.experimental import pallas as pl
from jax.experimental.pallas import tpu as pltpu
from jax.sharding import PartitionSpec as P

HEAD_DIM = 64
WINDOW = 256
POOL = 1024
BQ = 128
SPAN = BQ + 2 * WINDOW
TILES = SPAN // 128
STRIP = 16
NORM_ROWS = 512
PROJ_ROWS = 512
EDGE_ROWS = 512
OUT_ROWS = 256
HIDDEN = -1e30

VMEM = pl.BlockSpec(memory_space=pltpu.VMEM)
HBM = pl.BlockSpec(memory_space=pltpu.HBM)
SMEM = pl.BlockSpec(memory_space=pltpu.SMEM)
BF16 = jnp.bfloat16
F32 = jnp.float32


def sds(shape, dtype):
    return jax.ShapeDtypeStruct(shape, dtype)


def dot(a, b):
    return jnp.dot(a, b, preferred_element_type=F32)


def call(kernel, outs, *args, in_specs=None, out_specs=None, scratch=(), limit=24, flops=0, name=None):
    cost = pl.CostEstimate(flops=flops, bytes_accessed=4 << 20, transcendentals=0)
    return pl.pallas_call(
        kernel,
        out_shape=outs,
        in_specs=in_specs or [VMEM] * len(args),
        out_specs=out_specs or jax.tree.map(lambda _: VMEM, outs),
        scratch_shapes=scratch,
        compiler_params=pltpu.CompilerParams(vmem_limit_bytes=limit << 20),
        cost_estimate=cost,
        name=name,
    )(*args)


def rms(x, gain):
    return x * lax.rsqrt(jnp.mean(x * x, axis=-1, keepdims=True) + 1e-05) * gain


def head_ones(width):
    row = lax.broadcasted_iota(jnp.int32, (width, width), 0) // HEAD_DIM
    lane = lax.broadcasted_iota(jnp.int32, (width, width), 1) // HEAD_DIM
    return jnp.where(row == lane, 1.0 / HEAD_DIM, 0.0).astype(BF16)


def unit(x, ones):
    square = x * x
    high = square.astype(BF16)
    low = (square - high.astype(F32)).astype(BF16)
    mean = dot(high, ones) + dot(low, ones)
    return x * lax.rsqrt(mean + 1e-06)


def copy_in(pairs, sems):
    copies = [pltpu.make_async_copy(src, dst, sems.at[i]) for i, (src, dst) in enumerate(pairs)]
    for copy in copies:
        copy.start()
    return copies


def norm_kernel(
    tok_ref,
    gain_ref,
    coarse_gain_ref,
    normed_ref,
    coarse_ref,
    first_ref,
    second_ref,
    buf,
    gains,
    sems,
):
    rows = tok_ref.shape[0]
    count = rows // NORM_ROWS
    parts = [pl.ds(c * NORM_ROWS, NORM_ROWS) for c in range(count)]
    copies = copy_in(
        [(gain_ref, gains.at[0]), (coarse_gain_ref, gains.at[1])]
        + [(tok_ref.at[part], buf.at[part]) for part in parts],
        sems,
    )
    copies[0].wait()
    copies[1].wait()
    gain = gains[0]
    ones = jnp.ones((8, NORM_ROWS), BF16)
    pooled = []
    for c, part in enumerate(parts):
        copies[2 + c].wait()
        normed = rms(buf[part, :].astype(F32), gain).astype(BF16)
        normed_ref[part, :] = normed
        total = dot(ones, normed)[:1]
        if c * NORM_ROWS % POOL:
            pooled[-1] = pooled[-1] + total
        else:
            pooled.append(total)
    pooled = jnp.concatenate(pooled, 0) * (1.0 / POOL)
    last = jnp.where(lax.axis_index("seq") % 2 == 0, rows - WINDOW, 0)
    for ref, start in ((first_ref, last), (second_ref, rows - WINDOW - last)):
        ref[...] = normed_ref[pl.ds(pl.multiple_of(start, WINDOW), WINDOW), :]
    coarse_ref[...] = rms(pooled, gains[1]).astype(BF16)


def unit_columns(x):
    split = x.reshape(-1, HEAD_DIM, x.shape[1])
    mean = jnp.mean(split * split, axis=1, keepdims=True)
    return split * lax.rsqrt(mean + 1e-06)


def project_columns(weight, rows):
    return lax.dot_general(weight, rows, (((0,), (1,)), ((), ())), preferred_element_type=F32)


def row_parts(rows):
    return [pl.ds(start, PROJ_ROWS) for start in range(0, rows, PROJ_ROWS)]


def query_part(normed, w_ref, scale_ref, q_ref, part):
    q = unit_columns(project_columns(w_ref[...], normed))
    for h in range(q.shape[0]):
        factor = scale_ref[h] * HEAD_DIM ** (-0.5)
        q_ref[h * HEAD_DIM : (h + 1) * HEAD_DIM, part] = (q[h] * factor).astype(BF16)


def query_kernel(normed_ref, w_ref, scale_ref, q_ref):
    for part in row_parts(normed_ref.shape[0]):
        query_part(normed_ref[part, :], w_ref, scale_ref, q_ref, part)


def key_value_kernel(normed_ref, wk_ref, wv_ref, k_ref, v_ref):
    for part in row_parts(normed_ref.shape[0]):
        normed = normed_ref[part, :]
        k = unit_columns(project_columns(wk_ref[...], normed))
        k_ref[:, part] = k.reshape(k_ref.shape[0], PROJ_ROWS).astype(BF16)
        v_ref[part, :] = dot(normed, wv_ref[...]).astype(BF16)


def all_kernel(normed_ref, wk_ref, wv_ref, wq_ref, scale_ref, k_ref, v_ref, q_ref):
    key_value_kernel(normed_ref, wk_ref, wv_ref, k_ref, v_ref)
    query_kernel(normed_ref, wq_ref, scale_ref, q_ref)


def halo_kernel(first_ref, second_ref, wk_ref, wv_ref, k_ref, v_ref):
    odd = lax.axis_index("seq") % 2
    for ref, start in ((first_ref, (1 - odd) * WINDOW), (second_ref, odd * WINDOW)):
        part = pl.ds(pl.multiple_of(start, WINDOW), WINDOW)
        keys = unit_columns(project_columns(wk_ref[...], ref[...]))
        k_ref[:, part] = keys.reshape(k_ref.shape[0], WINDOW).astype(BF16)
        v_ref[part, :] = dot(ref[...], wv_ref[...]).astype(BF16)


def far_kernel(coarse_ref, wk_ref, wv_ref, k_ref, v_ref):
    count = coarse_ref.shape[0]
    coarse = coarse_ref[...]
    keys = unit(dot(coarse, wk_ref[...]), head_ones(v_ref.shape[1]))
    v_ref[...] = jnp.zeros_like(v_ref)
    v_ref[:count, :] = keys.astype(BF16)
    k_ref[...] = v_ref[...].T
    v_ref[:count, :] = dot(coarse, wv_ref[...]).astype(BF16)


def attention_kernel(far_count, edges, q_ref, main_k_ref, main_v_ref, *rest):
    if edges:
        halo_k_ref, halo_v_ref, *rest = rest
    far_k_ref, far_v_ref, o_ref, s_ref, p_ref, *rest = rest
    chunk = o_ref.shape[0]
    blocks = chunk // BQ
    width, rows = q_ref.shape
    heads = width // HEAD_DIM
    stack = heads * BQ
    far_width = far_v_ref.shape[0]
    far_tiles = far_width // 128
    tiles = TILES + far_tiles
    lane_head = lax.broadcasted_iota(jnp.int32, (BQ, width), 1) // HEAD_DIM
    seq_index = lax.axis_index("seq")
    is_first = seq_index == 0
    is_last = seq_index == lax.axis_size("seq") - 1
    side = chunk // 2 if edges else (rows - chunk) // 2

    if edges:
        k_ref, v_ref = rest
        inner = side + WINDOW
        k_ref[:, :WINDOW] = halo_k_ref[:, :WINDOW]
        v_ref[:WINDOW, :] = halo_v_ref[:WINDOW, :]
        k_ref[:, WINDOW : WINDOW + inner] = main_k_ref[:, :inner]
        v_ref[WINDOW : WINDOW + inner, :] = main_v_ref[:inner, :]
        k_ref[:, WINDOW + inner : WINDOW + 2 * inner] = main_k_ref[:, rows - inner :]
        v_ref[WINDOW + inner : WINDOW + 2 * inner, :] = main_v_ref[rows - inner :, :]
        k_ref[:, WINDOW + 2 * inner :] = halo_k_ref[:, WINDOW:]
        v_ref[WINDOW + 2 * inner :, :] = halo_v_ref[WINDOW:, :]
    else:
        k_ref, v_ref = main_k_ref, main_v_ref

    def at_second(b):
        return jnp.where(b >= blocks // 2, 1, 0)

    def query_rows(b):
        start = b * BQ + at_second(b) * (rows - chunk) if edges else side + b * BQ
        return pl.ds(pl.multiple_of(start, BQ), BQ)

    def key_rows(b):
        start = b * BQ + at_second(b) * 2 * WINDOW if edges else side - WINDOW + b * BQ
        return pl.ds(pl.multiple_of(start, BQ), SPAN)

    def scores(b, slot):
        q = q_ref[:, query_rows(b)].T
        queries = jnp.concatenate(
            [jnp.where(lane_head == h, q, jnp.zeros_like(q)) for h in range(heads)], 0
        )
        keys = jnp.concatenate([k_ref[:, key_rows(b)], far_k_ref[...]], 1)
        s_ref[slot] = dot(queries, keys)

    def hide_outside(b, slot):
        for edge, distance, near, outer in (
            (is_first, b, 1, 0),
            (is_last, blocks - 1 - b, TILES - 2, TILES - 1),
        ):
            for tile, reach in ((near, 1), (outer, 2)):

                @pl.when(edge & (distance < reach))
                def _():
                    s_ref[slot, :, tile * 128 : tile * 128 + 128] = jnp.full(
                        (stack, 128), HIDDEN, F32
                    )

    def softmax(slot):
        lane = lax.broadcasted_iota(jnp.int32, (STRIP, 128), 1)
        ahead = lane - lax.broadcasted_iota(jnp.int32, (STRIP, 128), 0)
        for r in range(0, stack, STRIP):
            at = r % BQ
            part = [s_ref[slot, r : r + STRIP, 128 * t : 128 * t + 128] for t in range(tiles)]
            part[0] = jnp.where(ahead >= at, part[0], HIDDEN)
            part[TILES - 1] = jnp.where(ahead <= at, part[TILES - 1], HIDDEN)
            if far_count < far_width:
                used = far_count - (far_tiles - 1) * 128
                part[-1] = jnp.where(lane < used, part[-1], HIDDEN)
            peak = jnp.max(functools.reduce(jnp.maximum, part), axis=1, keepdims=True)
            part = [jnp.exp(x - peak) for x in part]
            total = jnp.sum(functools.reduce(jnp.add, part), axis=1, keepdims=True)
            scale = 1.0 / total
            for t in range(tiles):
                p_ref[slot, r : r + STRIP, 128 * t : 128 * t + 128] = (part[t] * scale).astype(BF16)

    def mix(b, slot):
        values = jnp.concatenate([v_ref[key_rows(b), :], far_v_ref[...]], 0)
        mixed = dot(p_ref[slot], values)
        out = mixed[:BQ]
        for h in range(1, heads):
            out = jnp.where(lane_head == h, mixed[h * BQ : (h + 1) * BQ], out)
        o_ref[pl.ds(pl.multiple_of(b * BQ, BQ), BQ), :] = out.astype(BF16)

    def step(b, slot, mixes=True, scored=True):
        if edges:
            hide_outside(b, slot)
        if mixes:
            mix(b - 1, 1 - slot)
        if scored:
            scores(b + 1, 1 - slot)
        softmax(slot)

    scores(0, 0)
    step(0, 0, mixes=False)

    @pl.loop(0, (blocks - 2) // 2)
    def _(i):
        step(2 * i + 1, 1)
        step(2 * i + 2, 0)

    step(blocks - 1, 1, scored=False)
    mix(blocks - 1, 1)


def out_kernel(starts, own_ref, other_ref, w_ref, *rest):
    o_ref, buf, sems = rest[-3:]
    core = lax.axis_index("head")
    width = own_ref.shape[1]

    def weight(rows_of):
        rows = pl.ds(pl.multiple_of(rows_of * width, width), width)
        return w_ref[rows, pl.ds(pl.multiple_of(core * width, width), width)]

    both_w = jnp.concatenate([weight(core), weight(1 - core)], 0)
    copies = []
    for c in range(own_ref.shape[0] // OUT_ROWS):
        part = pl.ds(c * OUT_ROWS, OUT_ROWS)
        out = dot(jnp.concatenate([own_ref[part, :], other_ref[part, :]], 1), both_w)
        buf[part, :] = out.astype(BF16)
        target = o_ref.at[pl.ds(starts[c], OUT_ROWS)]
        copies.append(pltpu.make_async_copy(buf.at[part], target, sems.at[c]))
        copies[-1].start()
    for copy in copies:
        copy.wait()


def swap_heads(x):
    return lax.ppermute(x, "head", [(0, 1), (1, 0)])


def swap_pairs(x, start, seq_size):
    pairs = [(i, i + 1) for i in range(start, seq_size - 1, 2)]
    return lax.ppermute(x, "seq", pairs + [(b, a) for a, b in pairs])


def body(tokens, norm_gain, coarse_gain, w_query, w_key, w_value, w_out, score_scale):
    rows, full = tokens.shape
    heads = score_scale.shape[0]
    width = heads * HEAD_DIM
    seq_size = lax.axis_size("seq")
    pooled = rows // POOL
    power = seq_size & (seq_size - 1) == 0

    normed, coarse, first, second = call(
        norm_kernel,
        (
            sds((rows, full), BF16),
            sds((pooled, full), BF16),
            sds((WINDOW, full), BF16),
            sds((WINDOW, full), BF16),
        ),
        pltpu.with_memory_space_constraint(tokens, pltpu.HBM),
        pltpu.with_memory_space_constraint(norm_gain[None], pltpu.HBM),
        pltpu.with_memory_space_constraint(coarse_gain[None], pltpu.HBM),
        in_specs=[HBM] * 3,
        scratch=[
            pltpu.VMEM((rows, full), BF16),
            pltpu.VMEM((2, 1, full), F32),
            pltpu.SemaphoreType.DMA((rows // NORM_ROWS + 2,)),
        ],
        flops=2 << 30,
        name="norm",
    )
    columns = sds((width, rows), BF16)
    project = functools.partial(call, flops=4 << 30)

    def keys_values_of(x):
        outs = (columns, sds((rows, width), BF16))
        return project(key_value_kernel, outs, x, w_key, w_value, name="keys_values")

    def all_of(x):
        outs = (columns, sds((rows, width), BF16), columns)
        specs = [VMEM] * 4 + [SMEM]
        return project(
            all_kernel, outs, x, w_key, w_value, w_query, score_scale, in_specs=specs, name="all"
        )

    def queries_of(x):
        specs = [VMEM, VMEM, SMEM]
        return project(
            query_kernel, columns, x, w_query, score_scale, in_specs=specs, name="queries"
        )

    first_in = second_in = None
    pending = [keys_values_of, queries_of]
    covered = []
    steps = [1 << i for i in reversed(range(seq_size.bit_length() - 1))] if power else []
    while pending or steps:
        received = None
        if steps:
            step = steps.pop(0)
            pairs = [(i, i ^ step) for i in range(seq_size)]
            received = lax.ppermute(coarse, "seq", pairs)
        if pending:
            normed, coarse = lax.optimization_barrier((normed, coarse))
            result = pending.pop(0)(normed)
            if received is not None:
                received, result = lax.optimization_barrier((received, result))
            covered.append(result)
        if received is not None:
            coarse = jnp.concatenate([coarse, received], 0)
        if not pending and second_in is None:
            second, coarse = lax.optimization_barrier((second, coarse))
            first_in = swap_pairs(first, 0, seq_size)
            second_in = swap_pairs(second, 1, seq_size)
    (keys, values), queries = covered
    if not power:
        coarse = lax.all_gather(coarse, "seq", axis=0, tiled=True)
    far_count = coarse.shape[0]
    far_width = -(-far_count // 128) * 128
    far_keys, far_values = call(
        far_kernel,
        (sds((width, far_width), BF16), sds((far_width, width), BF16)),
        coarse,
        w_key,
        w_value,
        limit=16,
        name="far",
    )
    stack = heads * BQ
    scratch = [
        pltpu.VMEM((2, stack, SPAN + far_width), F32),
        pltpu.VMEM((2, stack, SPAN + far_width), BF16),
    ]
    attend = functools.partial(call, flops=10 << 30)
    middle = attend(
        functools.partial(attention_kernel, far_count, False),
        sds((rows - 2 * EDGE_ROWS, width), BF16),
        queries,
        keys,
        values,
        far_keys,
        far_values,
        scratch=scratch,
        name="middle",
    )
    middle_in = swap_heads(middle)
    first_in, second_in, middle = lax.optimization_barrier((first_in, second_in, middle))
    halo_keys, halo_values = call(
        halo_kernel,
        (sds((width, 2 * WINDOW), BF16), sds((2 * WINDOW, width), BF16)),
        first_in,
        second_in,
        w_key,
        w_value,
        limit=16,
        name="halo",
    )
    outer = attend(
        functools.partial(attention_kernel, far_count, True),
        sds((2 * EDGE_ROWS, width), BF16),
        queries,
        keys,
        values,
        halo_keys,
        halo_values,
        far_keys,
        far_values,
        scratch=scratch
        + [
            pltpu.VMEM((width, 2 * EDGE_ROWS + 4 * WINDOW), BF16),
            pltpu.VMEM((2 * EDGE_ROWS + 4 * WINDOW, width), BF16),
        ],
        name="outer",
    )
    outer_in = swap_heads(outer)
    last = rows - EDGE_ROWS
    spans = [
        (middle, middle_in, [*range(EDGE_ROWS, last, OUT_ROWS)]),
        (outer, outer_in, [*range(0, EDGE_ROWS, OUT_ROWS), *range(last, rows, OUT_ROWS)]),
    ]
    out = []
    for attended, swapped, starts in spans:
        out = [
            pl.pallas_call(
                functools.partial(out_kernel, starts),
                out_shape=sds((rows, width), BF16),
                in_specs=[VMEM] * 3 + [HBM] * len(out),
                out_specs=HBM,
                scratch_shapes=[
                    pltpu.VMEM(attended.shape, BF16),
                    pltpu.SemaphoreType.DMA((len(starts),)),
                ],
                input_output_aliases={3: 0} if out else {},
                compiler_params=pltpu.CompilerParams(vmem_limit_bytes=16 << 20),
                cost_estimate=pl.CostEstimate(
                    flops=1 << 30, bytes_accessed=4 << 20, transcendentals=0
                ),
                name="out",
            )(attended, swapped, w_out, *out)
        ]
    return out[0]


def solution(mesh):
    return jax.shard_map(
        body,
        mesh=mesh,
        in_specs=(
            P(("fields", "seq"), None),
            P(),
            P(),
            P(None, "head"),
            P(None, "head"),
            P(None, "head"),
            P(),
            P("head"),
        ),
        out_specs=P(("fields", "seq"), "head"),
        check_vma=False,
    )
```

```python
import functools

import jax
import jax.numpy as jnp
from jax import lax
from jax.experimental import pallas as pl
from jax.experimental.pallas import tpu as pltpu
from jax.sharding import PartitionSpec as P

HEAD_DIM = 64
WINDOW = 256
POOL = 1024
BQ = 128
SPAN = BQ + 2 * WINDOW
TILES = SPAN // 128
STRIP = 16
NORM_ROWS = 512
PROJ_ROWS = 512
EDGE_ROWS = 512
OUT_ROWS = 256
HIDDEN = -1e30

VMEM = pl.BlockSpec(memory_space=pltpu.VMEM)
HBM = pl.BlockSpec(memory_space=pltpu.HBM)
SMEM = pl.BlockSpec(memory_space=pltpu.SMEM)
BF16 = jnp.bfloat16
F32 = jnp.float32


def sds(shape, dtype):
    return jax.ShapeDtypeStruct(shape, dtype)


def dot(a, b):
    return jnp.dot(a, b, preferred_element_type=F32)


def call(kernel, outs, *args, in_specs=None, out_specs=None, scratch=(), limit=24, flops=0, name=None):
    cost = pl.CostEstimate(flops=flops, bytes_accessed=4 << 20, transcendentals=0)
    return pl.pallas_call(
        kernel,
        out_shape=outs,
        in_specs=in_specs or [VMEM] * len(args),
        out_specs=out_specs or jax.tree.map(lambda _: VMEM, outs),
        scratch_shapes=scratch,
        compiler_params=pltpu.CompilerParams(vmem_limit_bytes=limit << 20),
        cost_estimate=cost,
        name=name,
    )(*args)


def rms(x, gain):
    return x * lax.rsqrt(jnp.mean(x * x, axis=-1, keepdims=True) + 1e-05) * gain


def head_ones(width):
    row = lax.broadcasted_iota(jnp.int32, (width, width), 0) // HEAD_DIM
    lane = lax.broadcasted_iota(jnp.int32, (width, width), 1) // HEAD_DIM
    return jnp.where(row == lane, 1.0 / HEAD_DIM, 0.0).astype(BF16)


def unit(x, ones):
    square = x * x
    high = square.astype(BF16)
    low = (square - high.astype(F32)).astype(BF16)
    mean = dot(high, ones) + dot(low, ones)
    return x * lax.rsqrt(mean + 1e-06)


def copy_in(pairs, sems):
    copies = [pltpu.make_async_copy(src, dst, sems.at[i]) for i, (src, dst) in enumerate(pairs)]
    for copy in copies:
        copy.start()
    return copies


def norm_kernel(
    tok_ref,
    gain_ref,
    coarse_gain_ref,
    normed_ref,
    coarse_ref,
    first_ref,
    second_ref,
    buf,
    gains,
    sems,
):
    rows = tok_ref.shape[0]
    count = rows // NORM_ROWS
    parts = [pl.ds(c * NORM_ROWS, NORM_ROWS) for c in range(count)]
    copies = copy_in(
        [(gain_ref, gains.at[0]), (coarse_gain_ref, gains.at[1])]
        + [(tok_ref.at[part], buf.at[part]) for part in parts],
        sems,
    )
    copies[0].wait()
    copies[1].wait()
    gain = gains[0]
    ones = jnp.ones((8, NORM_ROWS), BF16)
    pooled = []
    for c, part in enumerate(parts):
        copies[2 + c].wait()
        normed = rms(buf[part, :].astype(F32), gain).astype(BF16)
        normed_ref[part, :] = normed
        total = dot(ones, normed)[:1]
        if c * NORM_ROWS % POOL:
            pooled[-1] = pooled[-1] + total
        else:
            pooled.append(total)
    pooled = jnp.concatenate(pooled, 0) * (1.0 / POOL)
    last = jnp.where(lax.axis_index("seq") % 2 == 0, rows - WINDOW, 0)
    for ref, start in ((first_ref, last), (second_ref, rows - WINDOW - last)):
        ref[...] = normed_ref[pl.ds(pl.multiple_of(start, WINDOW), WINDOW), :]
    coarse_ref[...] = rms(pooled, gains[1]).astype(BF16)


def unit_columns(x):
    split = x.reshape(-1, HEAD_DIM, x.shape[1])
    mean = jnp.mean(split * split, axis=1, keepdims=True)
    return split * lax.rsqrt(mean + 1e-06)


def project_columns(weight, rows):
    return lax.dot_general(weight, rows, (((0,), (1,)), ((), ())), preferred_element_type=F32)


def row_parts(rows):
    return [pl.ds(start, PROJ_ROWS) for start in range(0, rows, PROJ_ROWS)]


def query_part(normed, w_ref, scale_ref, q_ref, part):
    q = unit_columns(project_columns(w_ref[...], normed))
    for h in range(q.shape[0]):
        factor = scale_ref[h] * HEAD_DIM ** (-0.5)
        q_ref[h * HEAD_DIM : (h + 1) * HEAD_DIM, part] = (q[h] * factor).astype(BF16)


def query_kernel(normed_ref, w_ref, scale_ref, q_ref):
    for part in row_parts(normed_ref.shape[0]):
        query_part(normed_ref[part, :], w_ref, scale_ref, q_ref, part)


def key_value_kernel(normed_ref, wk_ref, wv_ref, k_ref, v_ref):
    for part in row_parts(normed_ref.shape[0]):
        normed = normed_ref[part, :]
        k = unit_columns(project_columns(wk_ref[...], normed))
        k_ref[:, part] = k.reshape(k_ref.shape[0], PROJ_ROWS).astype(BF16)
        v_ref[part, :] = dot(normed, wv_ref[...]).astype(BF16)


def all_kernel(normed_ref, wk_ref, wv_ref, wq_ref, scale_ref, k_ref, v_ref, q_ref):
    key_value_kernel(normed_ref, wk_ref, wv_ref, k_ref, v_ref)
    query_kernel(normed_ref, wq_ref, scale_ref, q_ref)


def far_kernel(coarse_ref, wk_ref, wv_ref, k_ref, v_ref):
    count = coarse_ref.shape[0]
    coarse = coarse_ref[...]
    keys = unit(dot(coarse, wk_ref[...]), head_ones(v_ref.shape[1]))
    v_ref[...] = jnp.zeros_like(v_ref)
    v_ref[:count, :] = keys.astype(BF16)
    k_ref[...] = v_ref[...].T
    v_ref[:count, :] = dot(coarse, wv_ref[...]).astype(BF16)


def attention_kernel(far_count, edges, q_ref, main_k_ref, main_v_ref, *rest):
    if edges:
        first_ref, second_ref, wk_ref, wv_ref, *rest = rest
    far_k_ref, far_v_ref, o_ref, s_ref, p_ref, *rest = rest
    chunk = o_ref.shape[0]
    blocks = chunk // BQ
    width, rows = q_ref.shape
    heads = width // HEAD_DIM
    stack = heads * BQ
    far_width = far_v_ref.shape[0]
    far_tiles = far_width // 128
    tiles = TILES + far_tiles
    lane_head = lax.broadcasted_iota(jnp.int32, (BQ, width), 1) // HEAD_DIM
    seq_index = lax.axis_index("seq")
    is_first = seq_index == 0
    is_last = seq_index == lax.axis_size("seq") - 1
    side = chunk // 2 if edges else (rows - chunk) // 2

    if edges:
        k_ref, v_ref = rest
        inner = side + WINDOW
        odd = seq_index % 2
        top = WINDOW + 2 * inner
        for ref, start in ((first_ref, (1 - odd) * top), (second_ref, odd * top)):
            part = pl.ds(pl.multiple_of(start, WINDOW), WINDOW)
            keys = unit_columns(project_columns(wk_ref[...], ref[...]))
            k_ref[:, part] = keys.reshape(width, WINDOW).astype(BF16)
            v_ref[part, :] = dot(ref[...], wv_ref[...]).astype(BF16)
        k_ref[:, WINDOW : WINDOW + inner] = main_k_ref[:, :inner]
        v_ref[WINDOW : WINDOW + inner, :] = main_v_ref[:inner, :]
        k_ref[:, WINDOW + inner : WINDOW + 2 * inner] = main_k_ref[:, rows - inner :]
        v_ref[WINDOW + inner : WINDOW + 2 * inner, :] = main_v_ref[rows - inner :, :]
    else:
        k_ref, v_ref = main_k_ref, main_v_ref

    def at_second(b):
        return jnp.where(b >= blocks // 2, 1, 0)

    def query_rows(b):
        start = b * BQ + at_second(b) * (rows - chunk) if edges else side + b * BQ
        return pl.ds(pl.multiple_of(start, BQ), BQ)

    def key_rows(b):
        start = b * BQ + at_second(b) * 2 * WINDOW if edges else side - WINDOW + b * BQ
        return pl.ds(pl.multiple_of(start, BQ), SPAN)

    def scores(b, slot):
        q = q_ref[:, query_rows(b)].T
        queries = jnp.concatenate(
            [jnp.where(lane_head == h, q, jnp.zeros_like(q)) for h in range(heads)], 0
        )
        keys = jnp.concatenate([k_ref[:, key_rows(b)], far_k_ref[...]], 1)
        s_ref[slot] = dot(queries, keys)

    def hide_outside(b, slot):
        for edge, distance, near, outer in (
            (is_first, b, 1, 0),
            (is_last, blocks - 1 - b, TILES - 2, TILES - 1),
        ):
            for tile, reach in ((near, 1), (outer, 2)):

                @pl.when(edge & (distance < reach))
                def _():
                    s_ref[slot, :, tile * 128 : tile * 128 + 128] = jnp.full(
                        (stack, 128), HIDDEN, F32
                    )

    def softmax(slot):
        lane = lax.broadcasted_iota(jnp.int32, (STRIP, 128), 1)
        ahead = lane - lax.broadcasted_iota(jnp.int32, (STRIP, 128), 0)
        for r in range(0, stack, STRIP):
            at = r % BQ
            part = [s_ref[slot, r : r + STRIP, 128 * t : 128 * t + 128] for t in range(tiles)]
            part[0] = jnp.where(ahead >= at, part[0], HIDDEN)
            part[TILES - 1] = jnp.where(ahead <= at, part[TILES - 1], HIDDEN)
            if far_count < far_width:
                used = far_count - (far_tiles - 1) * 128
                part[-1] = jnp.where(lane < used, part[-1], HIDDEN)
            peak = jnp.max(functools.reduce(jnp.maximum, part), axis=1, keepdims=True)
            part = [jnp.exp(x - peak) for x in part]
            total = jnp.sum(functools.reduce(jnp.add, part), axis=1, keepdims=True)
            scale = 1.0 / total
            for t in range(tiles):
                p_ref[slot, r : r + STRIP, 128 * t : 128 * t + 128] = (part[t] * scale).astype(BF16)

    def mix(b, slot):
        values = jnp.concatenate([v_ref[key_rows(b), :], far_v_ref[...]], 0)
        mixed = dot(p_ref[slot], values)
        out = mixed[:BQ]
        for h in range(1, heads):
            out = jnp.where(lane_head == h, mixed[h * BQ : (h + 1) * BQ], out)
        o_ref[pl.ds(pl.multiple_of(b * BQ, BQ), BQ), :] = out.astype(BF16)

    def step(b, slot, mixes=True, scored=True):
        if edges:
            hide_outside(b, slot)
        if mixes:
            mix(b - 1, 1 - slot)
        if scored:
            scores(b + 1, 1 - slot)
        softmax(slot)

    scores(0, 0)
    step(0, 0, mixes=False)

    @pl.loop(0, (blocks - 2) // 2)
    def _(i):
        step(2 * i + 1, 1)
        step(2 * i + 2, 0)

    step(blocks - 1, 1, scored=False)
    mix(blocks - 1, 1)


def out_kernel(starts, own_ref, other_ref, w_ref, *rest):
    o_ref, buf, sems = rest[-3:]
    core = lax.axis_index("head")
    width = own_ref.shape[1]

    def weight(rows_of):
        rows = pl.ds(pl.multiple_of(rows_of * width, width), width)
        return w_ref[rows, pl.ds(pl.multiple_of(core * width, width), width)]

    both_w = jnp.concatenate([weight(core), weight(1 - core)], 0)
    copies = []
    for c in range(own_ref.shape[0] // OUT_ROWS):
        part = pl.ds(c * OUT_ROWS, OUT_ROWS)
        out = dot(jnp.concatenate([own_ref[part, :], other_ref[part, :]], 1), both_w)
        buf[part, :] = out.astype(BF16)
        target = o_ref.at[pl.ds(starts[c], OUT_ROWS)]
        copies.append(pltpu.make_async_copy(buf.at[part], target, sems.at[c]))
        copies[-1].start()
    for copy in copies:
        copy.wait()


def swap_heads(x):
    return lax.ppermute(x, "head", [(0, 1), (1, 0)])


def swap_pairs(x, start, seq_size):
    pairs = [(i, i + 1) for i in range(start, seq_size - 1, 2)]
    return lax.ppermute(x, "seq", pairs + [(b, a) for a, b in pairs])


def body(tokens, norm_gain, coarse_gain, w_query, w_key, w_value, w_out, score_scale):
    rows, full = tokens.shape
    heads = score_scale.shape[0]
    width = heads * HEAD_DIM
    seq_size = lax.axis_size("seq")
    pooled = rows // POOL
    power = seq_size & (seq_size - 1) == 0

    normed, coarse, first, second = call(
        norm_kernel,
        (
            sds((rows, full), BF16),
            sds((pooled, full), BF16),
            sds((WINDOW, full), BF16),
            sds((WINDOW, full), BF16),
        ),
        pltpu.with_memory_space_constraint(tokens, pltpu.HBM),
        pltpu.with_memory_space_constraint(norm_gain[None], pltpu.HBM),
        pltpu.with_memory_space_constraint(coarse_gain[None], pltpu.HBM),
        in_specs=[HBM] * 3,
        scratch=[
            pltpu.VMEM((rows, full), BF16),
            pltpu.VMEM((2, 1, full), F32),
            pltpu.SemaphoreType.DMA((rows // NORM_ROWS + 2,)),
        ],
        flops=2 << 30,
        name="norm",
    )
    columns = sds((width, rows), BF16)
    project = functools.partial(call, flops=4 << 30)

    def keys_values_of(x):
        outs = (columns, sds((rows, width), BF16))
        return project(key_value_kernel, outs, x, w_key, w_value, name="keys_values")

    def all_of(x):
        outs = (columns, sds((rows, width), BF16), columns)
        specs = [VMEM] * 4 + [SMEM]
        return project(
            all_kernel, outs, x, w_key, w_value, w_query, score_scale, in_specs=specs, name="all"
        )

    def queries_of(x):
        specs = [VMEM, VMEM, SMEM]
        return project(
            query_kernel, columns, x, w_query, score_scale, in_specs=specs, name="queries"
        )

    first_in = second_in = None
    pending = [keys_values_of, queries_of]
    covered = []
    steps = [1 << i for i in reversed(range(seq_size.bit_length() - 1))] if power else []
    if len(steps) > 2:
        steps[0], steps[1] = steps[1], steps[0]
    while pending or steps:
        received = None
        if steps:
            step = steps.pop(0)
            pairs = [(i, i ^ step) for i in range(seq_size)]
            received = lax.ppermute(coarse, "seq", pairs)
        if pending:
            normed, coarse = lax.optimization_barrier((normed, coarse))
            result = pending.pop(0)(normed)
            if received is not None:
                received, result = lax.optimization_barrier((received, result))
            covered.append(result)
        if received is not None:
            coarse = jnp.concatenate([coarse, received], 0)
        if not pending and second_in is None:
            second, coarse = lax.optimization_barrier((second, coarse))
            first_in = swap_pairs(first, 0, seq_size)
            second_in = swap_pairs(second, 1, seq_size)
    (keys, values), queries = covered
    if not power:
        coarse = lax.all_gather(coarse, "seq", axis=0, tiled=True)
    far_count = coarse.shape[0]
    far_width = -(-far_count // 128) * 128
    far_keys, far_values = call(
        far_kernel,
        (sds((width, far_width), BF16), sds((far_width, width), BF16)),
        coarse,
        w_key,
        w_value,
        limit=16,
        name="far",
    )
    stack = heads * BQ
    scratch = [
        pltpu.VMEM((2, stack, SPAN + far_width), F32),
        pltpu.VMEM((2, stack, SPAN + far_width), BF16),
    ]
    attend = functools.partial(call, flops=10 << 30)
    middle = attend(
        functools.partial(attention_kernel, far_count, False),
        sds((rows - 2 * EDGE_ROWS, width), BF16),
        queries,
        keys,
        values,
        far_keys,
        far_values,
        scratch=scratch,
        name="middle",
    )
    middle_in = swap_heads(middle)
    first_in, second_in, middle = lax.optimization_barrier((first_in, second_in, middle))
    outer = attend(
        functools.partial(attention_kernel, far_count, True),
        sds((2 * EDGE_ROWS, width), BF16),
        queries,
        keys,
        values,
        first_in,
        second_in,
        w_key,
        w_value,
        far_keys,
        far_values,
        scratch=scratch
        + [
            pltpu.VMEM((width, 2 * EDGE_ROWS + 4 * WINDOW), BF16),
            pltpu.VMEM((2 * EDGE_ROWS + 4 * WINDOW, width), BF16),
        ],
        name="outer",
    )
    outer_in = swap_heads(outer)
    last = rows - EDGE_ROWS
    spans = [
        (middle, middle_in, [*range(EDGE_ROWS, last, OUT_ROWS)]),
        (outer, outer_in, [*range(0, EDGE_ROWS, OUT_ROWS), *range(last, rows, OUT_ROWS)]),
    ]
    out = []
    for attended, swapped, starts in spans:
        out = [
            pl.pallas_call(
                functools.partial(out_kernel, starts),
                out_shape=sds((rows, width), BF16),
                in_specs=[VMEM] * 3 + [HBM] * len(out),
                out_specs=HBM,
                scratch_shapes=[
                    pltpu.VMEM(attended.shape, BF16),
                    pltpu.SemaphoreType.DMA((len(starts),)),
                ],
                input_output_aliases={3: 0} if out else {},
                compiler_params=pltpu.CompilerParams(vmem_limit_bytes=16 << 20),
                cost_estimate=pl.CostEstimate(
                    flops=1 << 30, bytes_accessed=4 << 20, transcendentals=0
                ),
                name="out",
            )(attended, swapped, w_out, *out)
        ]
    return out[0]


def solution(mesh):
    return jax.shard_map(
        body,
        mesh=mesh,
        in_specs=(
            P(("fields", "seq"), None),
            P(),
            P(),
            P(None, "head"),
            P(None, "head"),
            P(None, "head"),
            P(),
            P("head"),
        ),
        out_specs=P(("fields", "seq"), "head"),
        check_vma=False,
    )
```

```python
import functools

import jax
import jax.numpy as jnp
from jax import lax
from jax.experimental import pallas as pl
from jax.experimental.pallas import tpu as pltpu
from jax.sharding import PartitionSpec as P

HEAD_DIM = 64
WINDOW = 256
POOL = 1024
BQ = 128
SPAN = BQ + 2 * WINDOW
TILES = SPAN // 128
STRIP = 16
NORM_ROWS = 512
PROJ_ROWS = 512
EDGE_ROWS = 512
OUT_ROWS = 256
HIDDEN = -1e30

VMEM = pl.BlockSpec(memory_space=pltpu.VMEM)
HBM = pl.BlockSpec(memory_space=pltpu.HBM)
SMEM = pl.BlockSpec(memory_space=pltpu.SMEM)
BF16 = jnp.bfloat16
F32 = jnp.float32


def sds(shape, dtype):
    return jax.ShapeDtypeStruct(shape, dtype)


def dot(a, b):
    return jnp.dot(a, b, preferred_element_type=F32)


def call(kernel, outs, *args, in_specs=None, out_specs=None, scratch=(), limit=24, flops=0, name=None):
    cost = pl.CostEstimate(flops=flops, bytes_accessed=4 << 20, transcendentals=0)
    return pl.pallas_call(
        kernel,
        out_shape=outs,
        in_specs=in_specs or [VMEM] * len(args),
        out_specs=out_specs or jax.tree.map(lambda _: VMEM, outs),
        scratch_shapes=scratch,
        compiler_params=pltpu.CompilerParams(vmem_limit_bytes=limit << 20),
        cost_estimate=cost,
        name=name,
    )(*args)


def rms(x, gain):
    return x * lax.rsqrt(jnp.mean(x * x, axis=-1, keepdims=True) + 1e-05) * gain


def head_ones(width):
    row = lax.broadcasted_iota(jnp.int32, (width, width), 0) // HEAD_DIM
    lane = lax.broadcasted_iota(jnp.int32, (width, width), 1) // HEAD_DIM
    return jnp.where(row == lane, 1.0 / HEAD_DIM, 0.0).astype(BF16)


def unit(x, ones):
    square = x * x
    high = square.astype(BF16)
    low = (square - high.astype(F32)).astype(BF16)
    mean = dot(high, ones) + dot(low, ones)
    return x * lax.rsqrt(mean + 1e-06)


def copy_in(pairs, sems):
    copies = [pltpu.make_async_copy(src, dst, sems.at[i]) for i, (src, dst) in enumerate(pairs)]
    for copy in copies:
        copy.start()
    return copies


def norm_kernel(
    tok_ref,
    gain_ref,
    coarse_gain_ref,
    normed_ref,
    coarse_ref,
    first_ref,
    second_ref,
    buf,
    gains,
    sems,
):
    rows = tok_ref.shape[0]
    count = rows // NORM_ROWS
    parts = [pl.ds(c * NORM_ROWS, NORM_ROWS) for c in range(count)]
    copies = copy_in(
        [(gain_ref, gains.at[0]), (coarse_gain_ref, gains.at[1])]
        + [(tok_ref.at[part], buf.at[part]) for part in parts],
        sems,
    )
    copies[0].wait()
    copies[1].wait()
    gain = gains[0]
    ones = jnp.ones((8, NORM_ROWS), BF16)
    pooled = []
    for c, part in enumerate(parts):
        copies[2 + c].wait()
        normed = rms(buf[part, :].astype(F32), gain).astype(BF16)
        normed_ref[part, :] = normed
        total = dot(ones, normed)[:1]
        if c * NORM_ROWS % POOL:
            pooled[-1] = pooled[-1] + total
        else:
            pooled.append(total)
    pooled = jnp.concatenate(pooled, 0) * (1.0 / POOL)
    last = jnp.where(lax.axis_index("seq") % 2 == 0, rows - WINDOW, 0)
    for ref, start in ((first_ref, last), (second_ref, rows - WINDOW - last)):
        ref[...] = normed_ref[pl.ds(pl.multiple_of(start, WINDOW), WINDOW), :]
    coarse_ref[...] = rms(pooled, gains[1]).astype(BF16)


def unit_columns(x):
    split = x.reshape(-1, HEAD_DIM, x.shape[1])
    mean = jnp.mean(split * split, axis=1, keepdims=True)
    return split * lax.rsqrt(mean + 1e-06)


def project_columns(weight, rows):
    return lax.dot_general(weight, rows, (((0,), (1,)), ((), ())), preferred_element_type=F32)


def row_parts(rows):
    return [pl.ds(start, PROJ_ROWS) for start in range(0, rows, PROJ_ROWS)]


def query_part(normed, w_ref, scale_ref, q_ref, part):
    q = unit_columns(project_columns(w_ref[...], normed))
    for h in range(q.shape[0]):
        factor = scale_ref[h] * HEAD_DIM ** (-0.5)
        q_ref[h * HEAD_DIM : (h + 1) * HEAD_DIM, part] = (q[h] * factor).astype(BF16)


def query_kernel(normed_ref, w_ref, scale_ref, q_ref):
    for part in row_parts(normed_ref.shape[0]):
        query_part(normed_ref[part, :], w_ref, scale_ref, q_ref, part)


def key_value_kernel(normed_ref, wk_ref, wv_ref, k_ref, v_ref):
    for part in row_parts(normed_ref.shape[0]):
        normed = normed_ref[part, :]
        k = unit_columns(project_columns(wk_ref[...], normed))
        k_ref[:, part] = k.reshape(k_ref.shape[0], PROJ_ROWS).astype(BF16)
        v_ref[part, :] = dot(normed, wv_ref[...]).astype(BF16)


def all_kernel(normed_ref, wk_ref, wv_ref, wq_ref, scale_ref, k_ref, v_ref, q_ref):
    key_value_kernel(normed_ref, wk_ref, wv_ref, k_ref, v_ref)
    query_kernel(normed_ref, wq_ref, scale_ref, q_ref)


def far_kernel(coarse_ref, wk_ref, wv_ref, k_ref, v_ref):
    count = coarse_ref.shape[0]
    coarse = coarse_ref[...]
    keys = unit(dot(coarse, wk_ref[...]), head_ones(v_ref.shape[1]))
    v_ref[...] = jnp.zeros_like(v_ref)
    v_ref[:count, :] = keys.astype(BF16)
    k_ref[...] = v_ref[...].T
    v_ref[:count, :] = dot(coarse, wv_ref[...]).astype(BF16)


def attention_kernel(far_count, edges, q_ref, main_k_ref, main_v_ref, *rest):
    if edges:
        first_ref, second_ref, wk_ref, wv_ref, *rest = rest
        far_k_ref, far_v_ref, o_ref, s_ref, p_ref, *rest = rest
    else:
        coarse_ref, wk_ref, wv_ref, o_ref, far_k_ref, far_v_ref, s_ref, p_ref = rest
        far_kernel(coarse_ref, wk_ref, wv_ref, far_k_ref, far_v_ref)
    chunk = o_ref.shape[0]
    blocks = chunk // BQ
    width, rows = q_ref.shape
    heads = width // HEAD_DIM
    stack = heads * BQ
    far_width = far_v_ref.shape[0]
    far_tiles = far_width // 128
    tiles = TILES + far_tiles
    lane_head = lax.broadcasted_iota(jnp.int32, (BQ, width), 1) // HEAD_DIM
    seq_index = lax.axis_index("seq")
    is_first = seq_index == 0
    is_last = seq_index == lax.axis_size("seq") - 1
    side = chunk // 2 if edges else (rows - chunk) // 2

    if edges:
        k_ref, v_ref = rest
        inner = side + WINDOW
        odd = seq_index % 2
        top = WINDOW + 2 * inner
        for ref, start in ((first_ref, (1 - odd) * top), (second_ref, odd * top)):
            part = pl.ds(pl.multiple_of(start, WINDOW), WINDOW)
            keys = unit_columns(project_columns(wk_ref[...], ref[...]))
            k_ref[:, part] = keys.reshape(width, WINDOW).astype(BF16)
            v_ref[part, :] = dot(ref[...], wv_ref[...]).astype(BF16)
        k_ref[:, WINDOW : WINDOW + inner] = main_k_ref[:, :inner]
        v_ref[WINDOW : WINDOW + inner, :] = main_v_ref[:inner, :]
        k_ref[:, WINDOW + inner : WINDOW + 2 * inner] = main_k_ref[:, rows - inner :]
        v_ref[WINDOW + inner : WINDOW + 2 * inner, :] = main_v_ref[rows - inner :, :]
    else:
        k_ref, v_ref = main_k_ref, main_v_ref

    def at_second(b):
        return jnp.where(b >= blocks // 2, 1, 0)

    def query_rows(b):
        start = b * BQ + at_second(b) * (rows - chunk) if edges else side + b * BQ
        return pl.ds(pl.multiple_of(start, BQ), BQ)

    def key_rows(b):
        start = b * BQ + at_second(b) * 2 * WINDOW if edges else side - WINDOW + b * BQ
        return pl.ds(pl.multiple_of(start, BQ), SPAN)

    def scores(b, slot):
        q = q_ref[:, query_rows(b)].T
        queries = jnp.concatenate(
            [jnp.where(lane_head == h, q, jnp.zeros_like(q)) for h in range(heads)], 0
        )
        keys = jnp.concatenate([k_ref[:, key_rows(b)], far_k_ref[...]], 1)
        s_ref[slot] = dot(queries, keys)

    def hide_outside(b, slot):
        for edge, distance, near, outer in (
            (is_first, b, 1, 0),
            (is_last, blocks - 1 - b, TILES - 2, TILES - 1),
        ):
            for tile, reach in ((near, 1), (outer, 2)):

                @pl.when(edge & (distance < reach))
                def _():
                    s_ref[slot, :, tile * 128 : tile * 128 + 128] = jnp.full(
                        (stack, 128), HIDDEN, F32
                    )

    def softmax(slot):
        lane = lax.broadcasted_iota(jnp.int32, (STRIP, 128), 1)
        ahead = lane - lax.broadcasted_iota(jnp.int32, (STRIP, 128), 0)
        for r in range(0, stack, STRIP):
            at = r % BQ
            part = [s_ref[slot, r : r + STRIP, 128 * t : 128 * t + 128] for t in range(tiles)]
            part[0] = jnp.where(ahead >= at, part[0], HIDDEN)
            part[TILES - 1] = jnp.where(ahead <= at, part[TILES - 1], HIDDEN)
            if far_count < far_width:
                used = far_count - (far_tiles - 1) * 128
                part[-1] = jnp.where(lane < used, part[-1], HIDDEN)
            peak = jnp.max(functools.reduce(jnp.maximum, part), axis=1, keepdims=True)
            part = [jnp.exp(x - peak) for x in part]
            total = jnp.sum(functools.reduce(jnp.add, part), axis=1, keepdims=True)
            scale = 1.0 / total
            for t in range(tiles):
                p_ref[slot, r : r + STRIP, 128 * t : 128 * t + 128] = (part[t] * scale).astype(BF16)

    def mix(b, slot):
        values = jnp.concatenate([v_ref[key_rows(b), :], far_v_ref[...]], 0)
        mixed = dot(p_ref[slot], values)
        out = mixed[:BQ]
        for h in range(1, heads):
            out = jnp.where(lane_head == h, mixed[h * BQ : (h + 1) * BQ], out)
        o_ref[pl.ds(pl.multiple_of(b * BQ, BQ), BQ), :] = out.astype(BF16)

    def step(b, slot, mixes=True, scored=True):
        if edges:
            hide_outside(b, slot)
        if mixes:
            mix(b - 1, 1 - slot)
        if scored:
            scores(b + 1, 1 - slot)
        softmax(slot)

    scores(0, 0)
    step(0, 0, mixes=False)

    @pl.loop(0, (blocks - 2) // 2)
    def _(i):
        step(2 * i + 1, 1)
        step(2 * i + 2, 0)

    step(blocks - 1, 1, scored=False)
    mix(blocks - 1, 1)


def out_kernel(starts, own_ref, other_ref, w_ref, *rest):
    o_ref, buf, sems = rest[-3:]
    core = lax.axis_index("head")
    width = own_ref.shape[1]

    def weight(rows_of):
        rows = pl.ds(pl.multiple_of(rows_of * width, width), width)
        return w_ref[rows, pl.ds(pl.multiple_of(core * width, width), width)]

    both_w = jnp.concatenate([weight(core), weight(1 - core)], 0)
    copies = []
    for c in range(own_ref.shape[0] // OUT_ROWS):
        part = pl.ds(c * OUT_ROWS, OUT_ROWS)
        out = dot(jnp.concatenate([own_ref[part, :], other_ref[part, :]], 1), both_w)
        buf[part, :] = out.astype(BF16)
        target = o_ref.at[pl.ds(starts[c], OUT_ROWS)]
        copies.append(pltpu.make_async_copy(buf.at[part], target, sems.at[c]))
        copies[-1].start()
    for copy in copies:
        copy.wait()


def swap_heads(x):
    return lax.ppermute(x, "head", [(0, 1), (1, 0)])


def swap_pairs(x, start, seq_size):
    pairs = [(i, i + 1) for i in range(start, seq_size - 1, 2)]
    return lax.ppermute(x, "seq", pairs + [(b, a) for a, b in pairs])


def body(tokens, norm_gain, coarse_gain, w_query, w_key, w_value, w_out, score_scale):
    rows, full = tokens.shape
    heads = score_scale.shape[0]
    width = heads * HEAD_DIM
    seq_size = lax.axis_size("seq")
    pooled = rows // POOL
    power = seq_size & (seq_size - 1) == 0

    normed, coarse, first, second = call(
        norm_kernel,
        (
            sds((rows, full), BF16),
            sds((pooled, full), BF16),
            sds((WINDOW, full), BF16),
            sds((WINDOW, full), BF16),
        ),
        pltpu.with_memory_space_constraint(tokens, pltpu.HBM),
        pltpu.with_memory_space_constraint(norm_gain[None], pltpu.HBM),
        pltpu.with_memory_space_constraint(coarse_gain[None], pltpu.HBM),
        in_specs=[HBM] * 3,
        scratch=[
            pltpu.VMEM((rows, full), BF16),
            pltpu.VMEM((2, 1, full), F32),
            pltpu.SemaphoreType.DMA((rows // NORM_ROWS + 2,)),
        ],
        flops=2 << 30,
        name="norm",
    )
    columns = sds((width, rows), BF16)
    project = functools.partial(call, flops=4 << 30)

    def keys_values_of(x):
        outs = (columns, sds((rows, width), BF16))
        return project(key_value_kernel, outs, x, w_key, w_value, name="keys_values")

    def all_of(x):
        outs = (columns, sds((rows, width), BF16), columns)
        specs = [VMEM] * 4 + [SMEM]
        return project(
            all_kernel, outs, x, w_key, w_value, w_query, score_scale, in_specs=specs, name="all"
        )

    def queries_of(x):
        specs = [VMEM, VMEM, SMEM]
        return project(
            query_kernel, columns, x, w_query, score_scale, in_specs=specs, name="queries"
        )

    first_in = second_in = None
    pending = [keys_values_of, queries_of]
    covered = []
    steps = [1 << i for i in reversed(range(seq_size.bit_length() - 1))] if power else []
    if len(steps) > 2:
        steps[0], steps[1] = steps[1], steps[0]
    while pending or steps:
        received = None
        if steps:
            step = steps.pop(0)
            pairs = [(i, i ^ step) for i in range(seq_size)]
            received = lax.ppermute(coarse, "seq", pairs)
        if pending:
            normed, coarse = lax.optimization_barrier((normed, coarse))
            result = pending.pop(0)(normed)
            if received is not None:
                received, result = lax.optimization_barrier((received, result))
            covered.append(result)
        if received is not None:
            coarse = jnp.concatenate([coarse, received], 0)
        if not pending and second_in is None:
            second, coarse = lax.optimization_barrier((second, coarse))
            first_in = swap_pairs(first, 0, seq_size)
            second_in = swap_pairs(second, 1, seq_size)
    (keys, values), queries = covered
    if not power:
        coarse = lax.all_gather(coarse, "seq", axis=0, tiled=True)
    far_count = coarse.shape[0]
    far_width = -(-far_count // 128) * 128
    stack = heads * BQ
    scratch = [
        pltpu.VMEM((2, stack, SPAN + far_width), F32),
        pltpu.VMEM((2, stack, SPAN + far_width), BF16),
    ]
    attend = functools.partial(call, flops=10 << 30)
    middle, far_keys, far_values = attend(
        functools.partial(attention_kernel, far_count, False),
        (
            sds((rows - 2 * EDGE_ROWS, width), BF16),
            sds((width, far_width), BF16),
            sds((far_width, width), BF16),
        ),
        queries,
        keys,
        values,
        coarse,
        w_key,
        w_value,
        scratch=scratch,
        name="middle",
    )
    middle_in = swap_heads(middle)
    first_in, second_in, middle = lax.optimization_barrier((first_in, second_in, middle))
    outer = attend(
        functools.partial(attention_kernel, far_count, True),
        sds((2 * EDGE_ROWS, width), BF16),
        queries,
        keys,
        values,
        first_in,
        second_in,
        w_key,
        w_value,
        far_keys,
        far_values,
        scratch=scratch
        + [
            pltpu.VMEM((width, 2 * EDGE_ROWS + 4 * WINDOW), BF16),
            pltpu.VMEM((2 * EDGE_ROWS + 4 * WINDOW, width), BF16),
        ],
        name="outer",
    )
    outer_in = swap_heads(outer)
    last = rows - EDGE_ROWS
    spans = [
        (middle, middle_in, [*range(EDGE_ROWS, last, OUT_ROWS)]),
        (outer, outer_in, [*range(0, EDGE_ROWS, OUT_ROWS), *range(last, rows, OUT_ROWS)]),
    ]
    out = []
    for attended, swapped, starts in spans:
        out = [
            pl.pallas_call(
                functools.partial(out_kernel, starts),
                out_shape=sds((rows, width), BF16),
                in_specs=[VMEM] * 3 + [HBM] * len(out),
                out_specs=HBM,
                scratch_shapes=[
                    pltpu.VMEM(attended.shape, BF16),
                    pltpu.SemaphoreType.DMA((len(starts),)),
                ],
                input_output_aliases={3: 0} if out else {},
                compiler_params=pltpu.CompilerParams(vmem_limit_bytes=16 << 20),
                cost_estimate=pl.CostEstimate(
                    flops=1 << 30, bytes_accessed=4 << 20, transcendentals=0
                ),
                name="out",
            )(attended, swapped, w_out, *out)
        ]
    return out[0]


def solution(mesh):
    return jax.shard_map(
        body,
        mesh=mesh,
        in_specs=(
            P(("fields", "seq"), None),
            P(),
            P(),
            P(None, "head"),
            P(None, "head"),
            P(None, "head"),
            P(),
            P("head"),
        ),
        out_specs=P(("fields", "seq"), "head"),
        check_vma=False,
    )
```
